128 devices in a mesh: replica: 16 (over x_lo, z, core), tensor: 8 (over y, x_hi).
Axes of the slice: x: 4 (x_hi: 2, x_lo: 2; x = x_hi * 2 + x_lo), y: 4, z: 4, core: 2. Of those that a mesh axis runs over, the one named last changes fastest.
Arguments:
- tokens: bfloat16 [8192, 1024], P('replica'), may hold values from -6 to 6
- targets: bfloat16 [8192, 1024], P('replica'), may hold values from -6 to 6
- row_ids: int32 [16, 3, 512], P('replica'), may hold values from 0 to 511
- anchor: float32 [2, 1024, 4096], P(None, None, 'tensor'), may hold values from -0.1875 to 0.1875
- momentum: float32 [16, 2, 1024, 4096], P('replica', None, None, 'tensor'), may hold values from -4 to 4
- slow: float32 [2, 1024, 4096], P(None, None, 'tensor'), may hold values from -6 to 6
Outputs:
- anchor_new: float32 [2, 1024, 4096], P(None, None, 'tensor')
- slow_new: float32 [2, 1024, 4096], P(None, None, 'tensor')
- momentum_new: float32 [16, 2, 1024, 4096], P('replica', None, None, 'tensor')
The draws below stay inside these ranges and needn't reach their ends.
Inputs may be any that keep to these rules, and one draw needn't show every extreme that they name: `row_ids`: each id names a row within its replica's own block of 512 rows; rows may repeat.
All inputs are finite; a program needn't handle non-finite values.
Results may differ from the reference program's by a relative error of at most 0.008.
Values may be sent and summed in bfloat16 or wider, within the bound.
A program may use at most 128 MiB of HBM per device.

```python
import jax
import jax.numpy as jnp
from jax import lax

D = 1024
FF = 4096
ROWS = 512
INNER = 3
REPLICAS = 16
TOKENS = 8192
N_REPLICA = 16


def with_ends(array, rng, least, top_value):
    longest = array.shape.index(max(array.shape))
    spots = []
    for shift in (0, 1):
        where = [jax.random.randint(jax.random.fold_in(rng, axis), (), 0, length) for axis, length in enumerate(array.shape)]
        where[longest] = (where[longest] + shift) % array.shape[longest]
        spots.append(tuple(where))
    return array.at[spots[0]].set(least).at[spots[1]].set(top_value)


def steps_of(own_key, dims, shards, least, largest):
    def one(position, shards_of):
        draws = jax.random.uniform(jax.random.fold_in(jax.random.fold_in(own_key, 6), position), (shards_of,), jnp.float32, least / len(shards), largest / len(shards))
        return jnp.repeat(jnp.exp(draws), dims[position] // shards_of).reshape((-1,) + (1,) * (len(dims) - position - 1))

    loudness = one(*shards[0])
    for cut in shards[1:]:
        loudness = loudness * one(*cut)
    return loudness


def bell_draw(key, shape, scale, limit, shards=(), kind=jnp.bfloat16):
    values = scale * jax.random.normal(key, shape, jnp.float32)
    if shards:
        values = values * steps_of(key, shape, shards, -0.22, 0.18)
    return jnp.clip(values, -limit, limit).astype(kind)


def setup_inputs(seed: int = 0) -> dict:
    splits = jax.random.split(jax.random.key(seed), 7)
    tokens = bell_draw(splits[0], (TOKENS, D), 1.0, 6.0, ((0, 16),))
    targets = bell_draw(splits[1], (TOKENS, D), 1.0, 6.0, ((0, 16),))
    row_ids = with_ends(jax.random.randint(splits[2], (REPLICAS, INNER, ROWS), 0, ROWS), jax.random.fold_in(splits[2], 1), 0, ROWS - 1).astype(jnp.int32)
    anchor = bell_draw(splits[3], (2, D, FF), D ** -0.5, 0.1875, ((2, 8),), jnp.float32)
    momentum = bell_draw(splits[4], (REPLICAS, 2, D, FF), 0.5, 4.0, ((0, 16), (3, 8)), jnp.float32)
    slow = bell_draw(splits[5], (2, D, FF), 1.0, 6.0, ((2, 8),), jnp.float32)
    return dict(tokens=tokens, targets=targets, row_ids=row_ids, anchor=anchor, momentum=momentum, slow=slow)


learn_rate = 0.02
inner_beta = 0.9
slow_beta = 0.5

def gelu_pair(pre):
    coeff = 0.7978845608028654
    inner = coeff * (pre + 0.044715 * pre * pre * pre)
    tanh_val = jnp.tanh(inner)
    value = 0.5 * pre * (1.0 + tanh_val)
    slope = 0.5 * (1.0 + tanh_val) + 0.5 * pre * (1.0 - tanh_val * tanh_val) * coeff * (1.0 + 3.0 * 0.044715 * pre * pre)
    return (value, slope)

def replica_grad(args):
    weights_bf, inputs, wanted = args
    pre = jnp.dot(inputs, weights_bf[0], preferred_element_type=jnp.float32)
    value, slope = gelu_pair(pre)
    hidden = value.astype(jnp.bfloat16)
    out = lax.dot_general(hidden, weights_bf[1], (((1,), (1,)), ((), ())), preferred_element_type=jnp.float32)
    error = ((out - wanted.astype(jnp.float32)) * (1.0 / ROWS)).astype(jnp.bfloat16)
    back = (jnp.dot(error, weights_bf[1], preferred_element_type=jnp.float32) * slope).astype(jnp.bfloat16)
    grad_in = lax.dot_general(inputs, back, (((0,), (0,)), ((), ())), preferred_element_type=jnp.float32)
    grad_out = lax.dot_general(error, hidden, (((0,), (0,)), ((), ())), preferred_element_type=jnp.float32)
    return jnp.stack([grad_in, grad_out])

def reference(tokens, targets, row_ids, anchor, momentum, slow):
    blocks_in = tokens.reshape(REPLICAS, ROWS, D)
    blocks_out = targets.reshape(REPLICAS, ROWS, D)
    weights = jnp.broadcast_to(anchor[None], (REPLICAS,) + anchor.shape).astype(jnp.float32)
    moment = momentum
    for step in range(INNER):
        if step > 0:
            incoming = jnp.roll(weights.astype(jnp.bfloat16), 2 ** (step - 1), axis=0)
            weights = 0.5 * (weights + incoming.astype(jnp.float32))
        picks = row_ids[:, step, :][:, :, None]
        inputs = jnp.take_along_axis(blocks_in, picks, axis=1)
        wanted = jnp.take_along_axis(blocks_out, picks, axis=1)
        weights_bf = weights.astype(jnp.bfloat16)
        grads = lax.map(replica_grad, (weights_bf, inputs, wanted))
        moment = inner_beta * moment + grads
        weights = weights - learn_rate * moment
    mean = lax.optimization_barrier(jnp.sum(weights, axis=0)) / N_REPLICA
    slow_new = slow_beta * slow + (anchor - mean) / learn_rate
    anchor_new = anchor - learn_rate * slow_new
    return (anchor_new, slow_new, moment)
```

```python
import jax
import jax.numpy as jnp
from jax import lax
from jax.sharding import PartitionSpec as P

INNER = 3


learn_rate = 0.02
inner_beta = 0.9
slow_beta = 0.5


def passed_along(block, axis, distance):
    devices = range(lax.axis_size(axis))
    route = [((i - distance) % len(devices), i) for i in devices]
    return lax.ppermute(block, axis, route)


def gelu_pair(pre):
    coeff = 0.7978845608028654
    inner = coeff * (pre + 0.044715 * pre * pre * pre)
    tanh_val = jnp.tanh(inner)
    value = 0.5 * pre * (1.0 + tanh_val)
    slope = 0.5 * (1.0 + tanh_val) + 0.5 * pre * (1.0 - tanh_val * tanh_val) * coeff * (
        1.0 + 3.0 * 0.044715 * pre * pre
    )
    return (value, slope)


def body(tokens, targets, row_ids, anchor, momentum, slow):
    row_count = tokens.shape[0]
    scale = 1.0 / row_count
    weights = anchor
    moment = momentum[0]
    parts = lax.axis_size("tensor")
    own = lax.axis_index("tensor")
    shard_rows = row_count // parts
    for step in range(INNER):
        if step > 0:
            incoming = passed_along(weights.astype(jnp.bfloat16), "replica", 2 ** (step - 1))
            weights = 0.5 * (weights + incoming.astype(jnp.float32))
        picks = row_ids[0, step]
        inputs = jnp.take(tokens, picks, axis=0)
        own_picks = lax.dynamic_slice(picks, (own * shard_rows,), (shard_rows,))
        wanted = jnp.take(targets, own_picks, axis=0)
        weights_bf = weights.astype(jnp.bfloat16)
        pre = jnp.dot(inputs, weights_bf[0], preferred_element_type=jnp.float32)
        value, slope = gelu_pair(pre)
        hidden = value.astype(jnp.bfloat16)
        partial_out = lax.dot_general(
            hidden, weights_bf[1], (((1,), (1,)), ((), ())), preferred_element_type=jnp.float32
        ).astype(jnp.bfloat16)
        summed = lax.psum_scatter(partial_out, "tensor", scatter_dimension=0, tiled=True)
        error = ((summed.astype(jnp.float32) - wanted.astype(jnp.float32)) * scale).astype(jnp.bfloat16)
        error = lax.all_gather(error, "tensor", axis=0, tiled=True)
        back = (jnp.dot(error, weights_bf[1], preferred_element_type=jnp.float32) * slope).astype(
            jnp.bfloat16
        )
        grad_in = lax.dot_general(
            inputs, back, (((0,), (0,)), ((), ())), preferred_element_type=jnp.float32
        )
        grad_out = lax.dot_general(
            error, hidden, (((0,), (0,)), ((), ())), preferred_element_type=jnp.float32
        )
        moment = inner_beta * moment + jnp.stack([grad_in, grad_out])
        weights = weights - learn_rate * moment
    replicas = lax.axis_size("replica")
    moved = ((anchor - weights) / learn_rate).astype(jnp.bfloat16)
    total = lax.psum_scatter(moved, "replica", scatter_dimension=1, tiled=True)
    total = lax.all_gather(total, "replica", axis=1, tiled=True)
    slow_new = slow_beta * slow + total.astype(jnp.float32) / replicas
    anchor_new = anchor - learn_rate * slow_new
    return (anchor_new, slow_new, moment[None])


def solution(mesh):
    return jax.shard_map(
        body,
        mesh=mesh,
        in_specs=(
            P("replica", None),
            P("replica", None),
            P("replica", None, None),
            P(None, None, "tensor"),
            P("replica", None, None, "tensor"),
            P(None, None, "tensor"),
        ),
        out_specs=(
            P(None, None, "tensor"),
            P(None, None, "tensor"),
            P("replica", None, None, "tensor"),
        ),
        check_vma=False,
    )
```

```python
import functools

import jax
import jax.numpy as jnp
from jax import lax
from jax.experimental import pallas as pl
from jax.experimental.pallas import tpu as pltpu
from jax.sharding import PartitionSpec as P

INNER = 3
learn_rate = 0.02
inner_beta = 0.9
slow_beta = 0.5

F32 = jnp.float32
BF16 = jnp.bfloat16
MESH = pl.DeviceIdType.MESH


def gelu_pair(pre):
    coeff = 0.7978845608028654
    square = pre * pre
    tanh_val = jnp.tanh(coeff * (pre + 0.044715 * pre * square))
    upper = 0.5 * (1.0 + tanh_val)
    value = pre * upper
    slope = upper + 0.5 * pre * (1.0 - tanh_val * tanh_val) * coeff * (
        1.0 + 3.0 * 0.044715 * square
    )
    return (value, slope)


def contract(a, b, dim_a, dim_b):
    return lax.dot_general(a, b, (((dim_a,), (dim_b,)), ((), ())), preferred_element_type=F32)


class Exchange:
    def __init__(self, pos, half, up, down, pair, block, part, hop, mid, fin, give, got, full, send, recv):
        self.pos, self.half, self.up, self.down, self.pair = pos, half, up, down, pair
        self.block, self.part, self.hop, self.mid, self.fin = block, part, hop, mid, fin
        self.give, self.got, self.full, self.send, self.recv = give, got, full, send, recv
        self.sent = []

    def copy(self, src, dst, index, device):
        return pltpu.make_async_remote_copy(
            src_ref=src,
            dst_ref=dst,
            send_sem=self.send.at[index],
            recv_sem=self.recv.at[index],
            device_id=device,
            device_id_type=MESH,
        )

    def start(self, src, dst, index, device):
        copy = self.copy(src, dst, index, device)
        copy.start()
        self.sent.append(copy)
        return copy

    def piece(self, chunk, half):
        return self.part.at[chunk, half]

    def reduce(self, make):
        pos = self.pos
        far, above, below = (pos + 2) % 4, (pos + 1) % 4, (pos + 3) % 4
        make(far)
        first_up = self.start(self.piece(far, 0), self.hop.at[0], 0, self.up)
        first_down = self.start(self.piece(far, 1), self.hop.at[1], 1, self.down)
        make(above)
        self.start(self.piece(above, 1), self.fin.at[1, 0], 2, self.up)
        make(below)
        self.start(self.piece(below, 0), self.fin.at[0, 0], 3, self.down)
        first_up.wait_recv()
        self.mid[0] = (self.part[above, 0].astype(F32) + self.hop[0].astype(F32)).astype(BF16)
        self.start(self.mid.at[0], self.fin.at[0, 1], 4, self.up)
        first_down.wait_recv()
        self.mid[1] = (self.part[below, 1].astype(F32) + self.hop[1].astype(F32)).astype(BF16)
        self.start(self.mid.at[1], self.fin.at[1, 1], 5, self.down)
        make(pos)
        for copy in self.sent[2:6]:
            copy.wait_recv()
        self.give[...] = self.total(1 - self.half).astype(BF16)
        last = self.start(self.give, self.got, 6, self.pair)
        mine = self.total(self.half)
        last.wait_recv()
        return mine + self.got[...].astype(F32)

    def total(self, half):
        return (
            self.part[self.pos, half].astype(F32)
            + self.fin[half, 0].astype(F32)
            + self.fin[half, 1].astype(F32)
        )

    def slot(self, chunk, half):
        return self.full.at[pl.ds(pl.multiple_of((chunk * 2 + half) * self.block, self.block), self.block)]

    def gather(self, arrived):
        pos, half = self.pos, self.half
        far, above, below = (pos + 2) % 4, (pos + 1) % 4, (pos + 3) % 4
        own, other = self.slot(pos, half), self.slot(pos, 1 - half)
        self.start(own, own, 7, self.pair)
        self.start(own, own, 8, self.up)
        self.start(own, own, 9, self.down)
        self.copy(other, other, 7, self.pair).wait_recv()
        self.start(other, other, 10, self.up)
        self.start(other, other, 11, self.down)
        arrived(pos)
        self.copy(own, self.slot(below, half), 8, self.up).wait_recv()
        self.copy(own, self.slot(above, half), 9, self.down).wait_recv()
        self.copy(own, self.slot(below, 1 - half), 10, self.up).wait_recv()
        self.copy(own, self.slot(above, 1 - half), 11, self.down).wait_recv()
        low, high = self.slot(below, 0), self.slot(above, 1)
        self.start(low, low, 12, self.up)
        self.start(high, high, 13, self.down)
        arrived(below)
        arrived(above)
        self.copy(own, self.slot(far, 0), 12, self.up).wait_recv()
        self.copy(own, self.slot(far, 1), 13, self.down).wait_recv()
        arrived(far)

    def finish(self):
        for copy in self.sent:
            copy.wait_send()


def kernel(
    ids, tokens, targets, anchor, momentum,
    moment_out, total_out,
    weights, moment, gone, cast, out_box, in_box, inputs, hidden, slope, back,
    part, hop, mid, fin, give, got, error,
    part2, hop2, mid2, fin2, give2, got2, total,
    send, recv, send2, recv2, box_send, box_recv, core_send, core_recv, local,
):
    rep, ten = lax.axis_index("replica"), lax.axis_index("tensor")
    row, side = ten // 2, ten % 2
    low, depth, core = rep // 8, (rep // 2) % 4, rep % 2
    up, down = (rep, (row + 1) % 4 * 2 + side), (rep, (row + 3) % 4 * 2 + side)
    pair = (rep, row * 2 + 1 - side)
    up2 = (low * 8 + (depth + 1) % 4 * 2 + core, ten)
    down2 = (low * 8 + (depth + 3) % 4 * 2 + core, ten)
    pair2 = ((1 - low) * 8 + depth * 2 + core, ten)
    twin = (low * 8 + depth * 2 + 1 - core, ten)

    load = [
        pltpu.make_async_copy(anchor.at[0], weights.at[0], local.at[0]),
        pltpu.make_async_copy(anchor.at[1], weights.at[1], local.at[1]),
        pltpu.make_async_copy(momentum.at[0], moment, local.at[2]),
    ]
    for copy in load:
        copy.start()

    barrier = pltpu.get_barrier_semaphore()
    peers = [up, down, pair, up2, down2, pair2, twin]
    peers += [((rep + shift) % 16, ten) for shift in (1, 2, 14, 15)]
    for peer in peers:
        pl.semaphore_signal(barrier, inc=1, device_id=peer, device_id_type=MESH)
    pl.semaphore_wait(barrier, len(peers))

    rows, width = inputs.shape
    units = hidden.shape[1]
    blocks = 4
    tall = width // blocks
    chunk_rows = rows // 4
    shard_rows = rows // 8

    def picked(step, start, count, table):
        chosen = ids[step, pl.ds(pl.multiple_of(start, shard_rows), count), :]
        lanes = lax.broadcasted_iota(jnp.int32, (count, rows), 1)
        mask = jnp.where(chosen == lanes, 1.0, 0.0).astype(BF16)
        return jnp.dot(mask, table[...], preferred_element_type=F32)

    def fetch(step):
        def some(i, carry):
            at = pl.ds(pl.multiple_of(i * chunk_rows, chunk_rows), chunk_rows)
            inputs[at, :] = picked(step, i * chunk_rows, chunk_rows, tokens).astype(BF16)
            return carry

        lax.fori_loop(0, 4, some, 0)

    fetch(0)

    def start_cast(i, carry):
        at = pl.ds(pl.multiple_of(i * 128, 128), 128)
        for m in (0, 1):
            cast[m, at, :] = weights[m, at, :].astype(BF16)
            gone[m, at, :] = jnp.zeros((128, units), F32)
        return carry

    load[0].wait()
    load[1].wait()
    lax.fori_loop(0, width // 128, start_cast, 0)
    load[2].wait()

    def box(step, m, j, device):
        at = pl.ds(pl.multiple_of(j * tall, tall), tall)
        return pltpu.make_async_remote_copy(
            src_ref=out_box.at[step, m, at],
            dst_ref=in_box.at[step, m, at],
            send_sem=box_send.at[step, m * blocks + j],
            recv_sem=box_recv.at[step, m * blocks + j],
            device_id=device,
            device_id_type=MESH,
        )

    def inner_step(step, carry):
        ring = Exchange(
            row, side, up, down, pair, shard_rows, part, hop.at[step], mid, fin.at[step],
            give, got.at[step], error.at[step], send.at[step], recv.at[step],
        )

        def make(chunk):
            at = pl.ds(pl.multiple_of(chunk * chunk_rows, chunk_rows), chunk_rows)
            pre = jnp.dot(inputs[at, :], cast[0], preferred_element_type=F32)
            value, rise = gelu_pair(pre)
            value = value.astype(BF16)
            hidden[at, :] = value
            slope[at, :] = rise
            out = contract(value, cast[1], 1, 1)
            part[chunk] = out.astype(BF16).reshape(2, shard_rows, width)

        summed = ring.reduce(make)
        wanted = picked(step, ten * shard_rows, shard_rows, targets)
        own = pl.ds(pl.multiple_of(ten * shard_rows, shard_rows), shard_rows)
        error[step, own, :] = ((summed - wanted) * (1.0 / rows)).astype(BF16)

        def arrived(chunk):
            at = pl.ds(pl.multiple_of(chunk * chunk_rows, chunk_rows), chunk_rows)
            slide = jnp.dot(error[step, at, :], cast[1], preferred_element_type=F32)
            back[at, :] = (slide * slope[at, :]).astype(BF16)

        ring.gather(arrived)

        def update(m, left, right):
            def one(j, carry):
                at = pl.ds(pl.multiple_of(j * tall, tall), tall)
                grad = contract(left[:, at], right[...], 0, 0)
                fresh = inner_beta * moment[m, at, :] + grad
                moment[m, at, :] = fresh
                moved = gone[m, at, :] + fresh
                gone[m, at, :] = moved
                kept = weights[m, at, :] - learn_rate * fresh
                weights[m, at, :] = kept
                out_box[step, m, at, :] = jnp.where(step < 2, kept, moved).astype(BF16)

                @pl.when(step < 2)
                def _():
                    box(step, m, j, ((rep + step + 1) % 16, ten)).start()

                @pl.when((step == 2) & (core == 1 - m))
                def _():
                    box(step, m, j, twin).start()

                return carry

            lax.fori_loop(0, blocks, one, 0)

        update(1, error.at[step], hidden)
        update(0, inputs, back)
        ring.finish()

        @pl.when(step < 2)
        def _():
            fetch(step + 1)
            for m in (1, 0):

                def mix(j, carry):
                    at = pl.ds(pl.multiple_of(j * tall, tall), tall)
                    box(step, m, j, ((rep + step + 1) % 16, ten)).wait_recv()
                    mixed = 0.5 * (weights[m, at, :] + in_box[step, m, at, :].astype(F32))
                    weights[m, at, :] = mixed
                    cast[m, at, :] = mixed.astype(BF16)
                    return carry

                lax.fori_loop(0, blocks, mix, 0)

            def drain(j, carry):
                for m in (1, 0):
                    box(step, m, j, ((rep + step + 1) % 16, ten)).wait_send()
                return carry

            lax.fori_loop(0, blocks, drain, 0)

        return carry

    lax.fori_loop(0, INNER, inner_step, 0)

    store = pltpu.make_async_copy(moment, moment_out.at[0], local.at[2])
    store.start()

    ring = Exchange(
        depth, low, up2, down2, pair2, width // 8, part2, hop2, mid2, fin2,
        give2, got2, total.at[core], send2, recv2,
    )

    def join(chunk):
        at = pl.ds(pl.multiple_of(chunk * tall, tall), tall)
        box(2, core, chunk, twin).wait_recv()
        both = gone[core, at, :] + in_box[2, core, at, :].astype(F32)
        part2[chunk] = both.astype(BF16).reshape(2, tall // 2, units)

    summed = ring.reduce(join)
    own = pl.ds(pl.multiple_of((depth * 2 + low) * (width // 8), width // 8), width // 8)
    total[core, own, :] = summed.astype(BF16)

    def across(which, chunk):
        at = pl.ds(pl.multiple_of(chunk * tall, tall), tall)
        return pltpu.make_async_remote_copy(
            src_ref=total.at[which, at],
            dst_ref=total.at[which, at],
            send_sem=core_send.at[chunk],
            recv_sem=core_recv.at[chunk],
            device_id=twin,
            device_id_type=MESH,
        )

    ring.gather(lambda chunk: across(core, chunk).start())
    for chunk in range(4):
        across(1 - core, chunk).wait_recv()
    save = pltpu.make_async_copy(total, total_out, local.at[0])
    save.start()
    for chunk in range(4):
        across(core, chunk).wait_send()
        box(2, 1 - core, chunk, twin).wait_send()
    ring.finish()
    save.wait()
    store.wait()


def body(tokens, targets, row_ids, anchor, momentum, slow):
    rows, width = tokens.shape
    units = anchor.shape[2]
    shard, wide = rows // 8, width // 8
    any_spec = pl.BlockSpec(memory_space=pl.ANY)
    vmem_spec = pl.BlockSpec(memory_space=pltpu.VMEM)
    dma = pltpu.SemaphoreType.DMA
    ids = row_ids.reshape(INNER, rows, 1)
    moment, total = pl.pallas_call(
        kernel,
        name="outer_round",
        out_shape=(
            jax.ShapeDtypeStruct(momentum.shape, F32),
            jax.ShapeDtypeStruct(anchor.shape, BF16),
        ),
        in_specs=[vmem_spec, vmem_spec, vmem_spec, any_spec, any_spec],
        out_specs=(any_spec, any_spec),
        scratch_shapes=[
            pltpu.VMEM((2, width, units), F32),
            pltpu.VMEM((2, width, units), F32),
            pltpu.VMEM((2, width, units), F32),
            pltpu.VMEM((2, width, units), BF16),
            pltpu.VMEM((INNER, 2, width, units), BF16),
            pltpu.VMEM((INNER, 2, width, units), BF16),
            pltpu.VMEM((rows, width), BF16),
            pltpu.VMEM((rows, units), BF16),
            pltpu.VMEM((rows, units), F32),
            pltpu.VMEM((rows, units), BF16),
            pltpu.VMEM((4, 2, shard, width), BF16),
            pltpu.VMEM((INNER, 2, shard, width), BF16),
            pltpu.VMEM((2, shard, width), BF16),
            pltpu.VMEM((INNER, 2, 2, shard, width), BF16),
            pltpu.VMEM((shard, width), BF16),
            pltpu.VMEM((INNER, shard, width), BF16),
            pltpu.VMEM((INNER, rows, width), BF16),
            pltpu.VMEM((4, 2, wide, units), BF16),
            pltpu.VMEM((2, wide, units), BF16),
            pltpu.VMEM((2, wide, units), BF16),
            pltpu.VMEM((2, 2, wide, units), BF16),
            pltpu.VMEM((wide, units), BF16),
            pltpu.VMEM((wide, units), BF16),
            pltpu.VMEM((2, width, units), BF16),
            dma((INNER, 14)),
            dma((INNER, 14)),
            dma((14,)),
            dma((14,)),
            dma((INNER, 8)),
            dma((INNER, 8)),
            dma((4,)),
            dma((4,)),
            dma((3,)),
        ],
        compiler_params=pltpu.CompilerParams(
            collective_id=0, has_side_effects=True, vmem_limit_bytes=60 * 1024 * 1024
        ),
    )(ids, tokens, targets, anchor, momentum)
    mean = total.astype(F32) * (1.0 / lax.axis_size("replica"))
    slow_new = slow_beta * slow + mean
    anchor_new = anchor - learn_rate * slow_new
    return (anchor_new, slow_new, moment)


def solution(mesh):
    return jax.shard_map(
        body,
        mesh=mesh,
        in_specs=(
            P("replica", None),
            P("replica", None),
            P("replica", None, None),
            P(None, None, "tensor"),
            P("replica", None, None, "tensor"),
            P(None, None, "tensor"),
        ),
        out_specs=(
            P(None, None, "tensor"),
            P(None, None, "tensor"),
            P("replica", None, None, "tensor"),
        ),
        check_vma=False,
    )
```

```python
import functools

import jax
import jax.numpy as jnp
from jax import lax
from jax.experimental import pallas as pl
from jax.experimental.pallas import tpu as pltpu
from jax.sharding import PartitionSpec as P

INNER = 3
learn_rate = 0.02
inner_beta = 0.9
slow_beta = 0.5

F32 = jnp.float32
BF16 = jnp.bfloat16
MESH = pl.DeviceIdType.MESH


def gelu_pair(pre):
    coeff = 0.7978845608028654
    square = pre * pre
    tanh_val = jnp.tanh(coeff * (pre + 0.044715 * pre * square))
    upper = 0.5 * (1.0 + tanh_val)
    value = pre * upper
    slope = upper + 0.5 * pre * (1.0 - tanh_val * tanh_val) * coeff * (
        1.0 + 3.0 * 0.044715 * square
    )
    return (value, slope)


def contract(a, b, dim_a, dim_b):
    return lax.dot_general(a, b, (((dim_a,), (dim_b,)), ((), ())), preferred_element_type=F32)


class Exchange:
    def __init__(self, pos, half, up, down, pair, block, part, hop, mid, fin, give, got, full, send, recv):
        self.pos, self.half, self.up, self.down, self.pair = pos, half, up, down, pair
        self.block, self.part, self.hop, self.mid, self.fin = block, part, hop, mid, fin
        self.give, self.got, self.full, self.send, self.recv = give, got, full, send, recv
        self.sent = []

    def copy(self, src, dst, index, device):
        return pltpu.make_async_remote_copy(
            src_ref=src,
            dst_ref=dst,
            send_sem=self.send.at[index],
            recv_sem=self.recv.at[index],
            device_id=device,
            device_id_type=MESH,
        )

    def start(self, src, dst, index, device):
        copy = self.copy(src, dst, index, device)
        copy.start()
        self.sent.append(copy)
        return copy

    def piece(self, chunk, half):
        return self.part.at[chunk, half]

    def reduce(self, make, early=None, idle=None):
        pos = self.pos
        far, above, below = (pos + 2) % 4, (pos + 1) % 4, (pos + 3) % 4
        make(far)
        first_up = self.start(self.piece(far, 0), self.hop.at[0], 0, self.up)
        first_down = self.start(self.piece(far, 1), self.hop.at[1], 1, self.down)
        if early is not None:
            early()
        make(above)
        self.start(self.piece(above, 1), self.fin.at[1, 0], 2, self.up)
        make(below)
        self.start(self.piece(below, 0), self.fin.at[0, 0], 3, self.down)
        make(pos)
        first_up.wait_recv()
        self.mid[0] = (self.part[above, 0].astype(F32) + self.hop[0].astype(F32)).astype(BF16)
        self.start(self.mid.at[0], self.fin.at[0, 1], 4, self.up)
        first_down.wait_recv()
        self.mid[1] = (self.part[below, 1].astype(F32) + self.hop[1].astype(F32)).astype(BF16)
        self.start(self.mid.at[1], self.fin.at[1, 1], 5, self.down)
        if idle is not None:
            idle()
        for copy in self.sent[2:6]:
            copy.wait_recv()
        self.give[...] = self.total(1 - self.half).astype(BF16)
        last = self.start(self.give, self.got, 6, self.pair)
        mine = self.total(self.half)
        last.wait_recv()
        return mine + self.got[...].astype(F32)

    def total(self, half):
        return (
            self.part[self.pos, half].astype(F32)
            + self.fin[half, 0].astype(F32)
            + self.fin[half, 1].astype(F32)
        )

    def slot(self, chunk, half):
        return self.full.at[pl.ds(pl.multiple_of((chunk * 2 + half) * self.block, self.block), self.block)]

    def gather(self, arrived, idle=None):
        pos, half = self.pos, self.half
        far, above, below = (pos + 2) % 4, (pos + 1) % 4, (pos + 3) % 4
        own, other = self.slot(pos, half), self.slot(pos, 1 - half)
        self.start(own, own, 7, self.pair)
        self.start(own, own, 8, self.up)
        self.start(own, own, 9, self.down)
        if idle is not None:
            idle(0)
        self.copy(other, other, 7, self.pair).wait_recv()
        self.start(other, other, 10, self.up)
        self.start(other, other, 11, self.down)
        arrived(pos, 0)
        early, late = self.slot(below, half), self.slot(above, 1 - half)
        self.copy(own, early, 8, self.up).wait_recv()
        self.start(early, early, 12, self.up)
        if idle is not None:
            idle(1)
        self.copy(own, late, 11, self.down).wait_recv()
        self.start(late, late, 13, self.down)
        self.copy(own, self.slot(above, half), 9, self.down).wait_recv()
        arrived(above, 1)
        self.copy(own, self.slot(below, 1 - half), 10, self.up).wait_recv()
        arrived(below, 2)
        self.copy(own, self.slot(far, half), 12, self.up).wait_recv()
        self.copy(own, self.slot(far, 1 - half), 13, self.down).wait_recv()
        arrived(far, 3)

    def finish(self):
        for copy in self.sent:
            copy.wait_send()


def kernel(
    ids, tokens, targets, anchor, momentum,
    moment_out, total_out,
    weights, moment, gone, cast, out_box, in_box, twin_out, twin_in,
    inputs, hidden, slope, back, want,
    near_inputs, near_hidden, near_slope, near_back, near_error, relay,
    part, hop, mid, fin, give, got, error,
    part2, hop2, mid2, fin2, give2, got2, total,
    send, recv, send2, recv2, box_send, box_recv, near_send, near_recv,
    relay_send, relay_recv, twin_send, twin_recv, core_send, core_recv, local,
):
    rep, ten = lax.axis_index("replica"), lax.axis_index("tensor")
    row, side = ten // 2, ten % 2
    low, depth, core = rep // 8, (rep // 2) % 4, rep % 2

    def plane(shift):
        return low * 8 + (depth + shift) % 4 * 2 + core

    up, down = (rep, (row + 1) % 4 * 2 + side), (rep, (row + 3) % 4 * 2 + side)
    pair = (rep, row * 2 + 1 - side)
    up2, down2 = (plane(1), ten), (plane(3), ten)
    pair2 = ((1 - low) * 8 + depth * 2 + core, ten)
    twin = (low * 8 + depth * 2 + 1 - core, ten)
    after, second = ((rep + 1) % 16, ten), ((rep + 2) % 16, ten)
    relay_end = ((plane(2) + 2) % 16, ten)
    past = (rep + 14) % 16
    relay_start = (past // 8 * 8 + ((past // 2) % 4 + 2) % 4 * 2 + core, ten)

    load = [
        pltpu.make_async_copy(anchor.at[0], weights.at[0], local.at[0]),
        pltpu.make_async_copy(anchor.at[1], weights.at[1], local.at[1]),
        pltpu.make_async_copy(momentum.at[0], moment, local.at[2]),
    ]
    for copy in load:
        copy.start()

    barrier = pltpu.get_barrier_semaphore()
    peers = [up, down, pair, up2, down2, pair2, twin, relay_end, relay_start]
    peers += [((rep + shift) % 16, ten) for shift in (1, 2, 14, 15)]
    for peer in peers:
        pl.semaphore_signal(barrier, inc=1, device_id=peer, device_id_type=MESH)
    pl.semaphore_wait(barrier, len(peers))

    rows, width = inputs.shape
    units = hidden.shape[1]
    blocks = 4
    tall = width // blocks
    chunk_rows = rows // 4
    shard_rows = rows // 8

    def remote(src, dst, send_sem, recv_sem, device):
        return pltpu.make_async_remote_copy(
            src_ref=src, dst_ref=dst, send_sem=send_sem, recv_sem=recv_sem,
            device_id=device, device_id_type=MESH,
        )

    def chunk_at(chunk):
        return pl.ds(pl.multiple_of(chunk * chunk_rows, chunk_rows), chunk_rows)

    def block_at(j):
        return pl.ds(pl.multiple_of(j * tall, tall), tall)

    def picked(step, chunk, table):
        chosen = ids[step, :, chunk_at(chunk)]
        places = lax.broadcasted_iota(jnp.int32, (rows, chunk_rows), 0)
        mask = jnp.where(chosen == places, 1.0, 0.0).astype(BF16)
        return contract(mask, table[...], 0, 0)

    def fetch(step):
        def some(i, carry):
            inputs[chunk_at(i), :] = picked(step, i, tokens).astype(BF16)
            return carry

        lax.fori_loop(0, 4, some, 0)

    def start_cast(i, carry):
        at = pl.ds(pl.multiple_of(i * 128, 128), 128)
        for m in (0, 1):
            cast[m, at, :] = weights[m, at, :].astype(BF16)
        return carry

    def decay(i, carry):
        at = pl.ds(pl.multiple_of(i * 128, 128), 128)
        for m in (0, 1):
            out_box[0, m, at, :] = (inner_beta * moment[m, at, :]).astype(BF16)
        return carry

    near_x = remote(inputs, near_inputs, near_send.at[4], near_recv.at[4], after)
    near_m = remote(out_box.at[0], in_box.at[0], near_send.at[5], near_recv.at[5], after)

    def near_piece(chunk, order):
        at = chunk_at(chunk)
        return remote(
            error.at[0, at], near_error.at[at], near_send.at[order], near_recv.at[order], after
        )

    def box(m, j):
        at = block_at(j)
        index = m * blocks + j
        return remote(
            out_box.at[1, m, at], in_box.at[1, m, at], box_send.at[index], box_recv.at[index], second
        )

    def leg(hop_index, j):
        src = out_box.at[1, 1, block_at(j)] if hop_index == 0 else relay.at[hop_index - 1, j]
        dst = in_box.at[1, 1, block_at(j)] if hop_index == 2 else relay.at[hop_index, j]
        return remote(
            src, dst, relay_send.at[hop_index, j], relay_recv.at[hop_index, j],
            relay_end if hop_index == 2 else down2,
        )

    def twin_box(j):
        at = block_at(j)
        return remote(twin_out.at[at], twin_in.at[at], twin_send.at[j], twin_recv.at[j], twin)

    fetch(0)
    near_x.start()
    load[0].wait()
    load[1].wait()
    lax.fori_loop(0, width // 128, start_cast, 0)

    def one_step(step):
        ring = Exchange(
            row, side, up, down, pair, shard_rows, part, hop.at[step], mid, fin.at[step],
            give, got.at[step], error.at[step], send.at[step], recv.at[step],
        )

        def forward(source, at, kept, rise):
            pre = jnp.dot(source[at, :], cast[0], preferred_element_type=F32)
            value, tilt = gelu_pair(pre)
            value = value.astype(BF16)
            kept[at, :] = value
            rise[at, :] = tilt
            return value

        def make(chunk):
            value = forward(inputs, chunk_at(chunk), hidden, slope)
            out = contract(value, cast[1], 1, 1)
            part[chunk] = out.astype(BF16).reshape(2, shard_rows, width)

        def early():
            load[2].wait()
            lax.fori_loop(0, width // 128, decay, 0)
            near_m.start()

        def idle():
            want[...] = picked(step, row, targets).reshape(2, shard_rows, width)

        summed = ring.reduce(make, early if step == 0 else None, idle)
        own = pl.ds(pl.multiple_of(ten * shard_rows, shard_rows), shard_rows)
        error[step, own, :] = ((summed - want[side]) * (1.0 / rows)).astype(BF16)

        def pull(source, at, rise, result):
            slide = jnp.dot(source[at, :], cast[1], preferred_element_type=F32)
            result[at, :] = (slide * rise[at, :]).astype(BF16)

        def arrived(chunk, order):
            if step == 0:
                near_piece(chunk, order).start()
            pull(error.at[step], chunk_at(chunk), slope, back)

        def near_forward(part_of):
            if part_of == 0:
                near_x.wait_recv()

            def one(i, carry):
                forward(near_inputs, chunk_at(i), near_hidden, near_slope)
                return carry

            lax.fori_loop(part_of * 2, part_of * 2 + 2, one, 0)

        ring.gather(arrived, near_forward if step == 0 else None)

        def update(m, left, right, first, last, ship):
            def one(j, carry):
                at = block_at(j)
                fresh = inner_beta * moment[m, at, :] + contract(left[:, at], right[...], 0, 0)
                moment[m, at, :] = fresh
                moved = fresh if step == 0 else gone[m, at, :] + fresh
                gone[m, at, :] = moved
                if step < 2:
                    kept = weights[m, at, :] - learn_rate * fresh
                    weights[m, at, :] = kept
                if step == 1:
                    out_box[1, m, at, :] = kept.astype(BF16)
                    ship(j).start()
                if step == 2:

                    @pl.when(core == 1 - m)
                    def _():
                        twin_out[at, :] = moved.astype(BF16)
                        twin_box(j).start()

                return carry

            lax.fori_loop(first, last, one, 0)

        def blend(m, at, other):
            mixed = 0.5 * (weights[m, at, :] + other)
            weights[m, at, :] = mixed
            cast[m, at, :] = mixed.astype(BF16)

        if step == 1:
            update(1, error.at[step], hidden, 0, 2, lambda j: leg(0, j))
            update(1, error.at[step], hidden, 2, 4, lambda j: box(1, j))
            update(0, inputs, back, 0, 4, lambda j: box(0, j))
        else:
            update(1, error.at[step], hidden, 0, 4, None)
            update(0, inputs, back, 0, 4, None)
        ring.finish()

        if step == 0:
            far, above, below = (row + 2) % 4, (row + 1) % 4, (row + 3) % 4
            for order, chunk in enumerate((row, above, below, far)):
                near_piece(chunk, order).wait_recv()
                pull(near_error, chunk_at(chunk), near_slope, near_back)
            near_m.wait_recv()
            near_x.wait_send()
            for m, left, right in ((1, near_error, near_hidden), (0, near_inputs, near_back)):

                def one(j, carry):
                    at = block_at(j)
                    grad = contract(left[:, at], right[...], 0, 0)
                    began = weights[m, at, :] + learn_rate * moment[m, at, :]
                    near = began - learn_rate * (in_box[0, m, at, :].astype(F32) + grad)
                    blend(m, at, near.astype(BF16).astype(F32))
                    return carry

                lax.fori_loop(0, blocks, one, 0)
            fetch(1)
            near_m.wait_send()
            for order, chunk in enumerate((row, above, below, far)):
                near_piece(chunk, order).wait_send()

        if step == 1:

            def take(m, j, copy):
                copy.wait_recv()
                blend(m, block_at(j), in_box[1, m, block_at(j), :].astype(F32))

            def relay_on(hop_index, j):
                leg(hop_index, j).wait_recv()
                leg(hop_index + 1, j).start()

            fetch(2)
            relay_on(0, 0)
            take(1, 2, box(1, 2))
            relay_on(0, 1)
            take(1, 3, box(1, 3))
            relay_on(1, 0)
            take(0, 0, box(0, 0))
            relay_on(1, 1)
            take(0, 1, box(0, 1))
            take(1, 0, leg(2, 0))
            take(0, 2, box(0, 2))
            take(1, 1, leg(2, 1))
            take(0, 3, box(0, 3))
            for m, j in ((1, 2), (1, 3), (0, 0), (0, 1), (0, 2), (0, 3)):
                box(m, j).wait_send()
            for hop_index in range(3):
                for j in (0, 1):
                    leg(hop_index, j).wait_send()

    for step in range(INNER):
        one_step(step)

    store = pltpu.make_async_copy(moment, moment_out.at[0], local.at[2])
    store.start()

    ring = Exchange(
        depth, low, up2, down2, pair2, width // 8, part2, hop2, mid2, fin2,
        give2, got2, total.at[core], send2, recv2,
    )

    def join(chunk):
        at = pl.ds(pl.multiple_of(chunk * tall, tall), tall)
        twin_box(chunk).wait_recv()
        both = gone[core, at, :] + twin_in[at, :].astype(F32)
        part2[chunk] = both.astype(BF16).reshape(2, tall // 2, units)

    summed = ring.reduce(join)
    own = pl.ds(pl.multiple_of((depth * 2 + low) * (width // 8), width // 8), width // 8)
    total[core, own, :] = summed.astype(BF16)

    def across(which, chunk):
        at = pl.ds(pl.multiple_of(chunk * tall, tall), tall)
        return pltpu.make_async_remote_copy(
            src_ref=total.at[which, at],
            dst_ref=total.at[which, at],
            send_sem=core_send.at[chunk],
            recv_sem=core_recv.at[chunk],
            device_id=twin,
            device_id_type=MESH,
        )

    ring.gather(lambda chunk, order: across(core, chunk).start())
    for chunk in range(4):
        across(1 - core, chunk).wait_recv()
    save = pltpu.make_async_copy(total, total_out, local.at[0])
    save.start()
    for chunk in range(4):
        across(core, chunk).wait_send()
        twin_box(chunk).wait_send()
    ring.finish()
    save.wait()
    store.wait()


def body(tokens, targets, row_ids, anchor, momentum, slow):
    rows, width = tokens.shape
    units = anchor.shape[2]
    shard, wide = rows // 8, width // 8
    any_spec = pl.BlockSpec(memory_space=pl.ANY)
    vmem_spec = pl.BlockSpec(memory_space=pltpu.VMEM)
    dma = pltpu.SemaphoreType.DMA
    ids = row_ids.reshape(INNER, 1, rows)
    moment, total = pl.pallas_call(
        kernel,
        name="outer_round",
        out_shape=(
            jax.ShapeDtypeStruct(momentum.shape, F32),
            jax.ShapeDtypeStruct(anchor.shape, BF16),
        ),
        in_specs=[vmem_spec, vmem_spec, vmem_spec, any_spec, any_spec],
        out_specs=(any_spec, any_spec),
        scratch_shapes=[
            pltpu.VMEM((2, width, units), F32),
            pltpu.VMEM((2, width, units), F32),
            pltpu.VMEM((2, width, units), F32),
            pltpu.VMEM((2, width, units), BF16),
            pltpu.VMEM((2, 2, width, units), BF16),
            pltpu.VMEM((2, 2, width, units), BF16),
            pltpu.VMEM((width, units), BF16),
            pltpu.VMEM((width, units), BF16),
            pltpu.VMEM((rows, width), BF16),
            pltpu.VMEM((rows, units), BF16),
            pltpu.VMEM((rows, units), F32),
            pltpu.VMEM((rows, units), BF16),
            pltpu.VMEM((2, shard, width), F32),
            pltpu.VMEM((rows, width), BF16),
            pltpu.VMEM((rows, units), BF16),
            pltpu.VMEM((rows, units), F32),
            pltpu.VMEM((rows, units), BF16),
            pltpu.VMEM((rows, width), BF16),
            pltpu.VMEM((2, 2, width // 4, units), BF16),
            pltpu.VMEM((4, 2, shard, width), BF16),
            pltpu.VMEM((INNER, 2, shard, width), BF16),
            pltpu.VMEM((2, shard, width), BF16),
            pltpu.VMEM((INNER, 2, 2, shard, width), BF16),
            pltpu.VMEM((shard, width), BF16),
            pltpu.VMEM((INNER, shard, width), BF16),
            pltpu.VMEM((INNER, rows, width), BF16),
            pltpu.VMEM((4, 2, wide, units), BF16),
            pltpu.VMEM((2, wide, units), BF16),
            pltpu.VMEM((2, wide, units), BF16),
            pltpu.VMEM((2, 2, wide, units), BF16),
            pltpu.VMEM((wide, units), BF16),
            pltpu.VMEM((wide, units), BF16),
            pltpu.VMEM((2, width, units), BF16),
            dma((INNER, 14)),
            dma((INNER, 14)),
            dma((14,)),
            dma((14,)),
            dma((8,)),
            dma((8,)),
            dma((6,)),
            dma((6,)),
            dma((3, 2)),
            dma((3, 2)),
            dma((4,)),
            dma((4,)),
            dma((4,)),
            dma((4,)),
            dma((3,)),
        ],
        compiler_params=pltpu.CompilerParams(
            collective_id=0, has_side_effects=True, vmem_limit_bytes=60 * 1024 * 1024
        ),
    )(ids, tokens, targets, anchor, momentum)
    mean = total.astype(F32) * (1.0 / lax.axis_size("replica"))
    slow_new = slow_beta * slow + mean
    anchor_new = anchor - learn_rate * slow_new
    return (anchor_new, slow_new, moment)


def solution(mesh):
    return jax.shard_map(
        body,
        mesh=mesh,
        in_specs=(
            P("replica", None),
            P("replica", None),
            P("replica", None, None),
            P(None, None, "tensor"),
            P("replica", None, None, "tensor"),
            P(None, None, "tensor"),
        ),
        out_specs=(
            P(None, None, "tensor"),
            P(None, None, "tensor"),
            P("replica", None, None, "tensor"),
        ),
        check_vma=False,
    )
```

```python
import functools

import jax
import jax.numpy as jnp
from jax import lax
from jax.experimental import pallas as pl
from jax.experimental.pallas import tpu as pltpu
from jax.sharding import PartitionSpec as P

INNER = 3
learn_rate = 0.02
inner_beta = 0.9
slow_beta = 0.5

F32 = jnp.float32
BF16 = jnp.bfloat16
MESH = pl.DeviceIdType.MESH


def gelu_pair(pre):
    coeff = 0.7978845608028654
    square = pre * pre
    tanh_val = jnp.tanh(coeff * (pre + 0.044715 * pre * square))
    upper = 0.5 * (1.0 + tanh_val)
    value = pre * upper
    slope = upper + 0.5 * pre * (1.0 - tanh_val * tanh_val) * coeff * (
        1.0 + 3.0 * 0.044715 * square
    )
    return (value, slope)


def contract(a, b, dim_a, dim_b):
    return lax.dot_general(a, b, (((dim_a,), (dim_b,)), ((), ())), preferred_element_type=F32)


class Exchange:
    def __init__(self, pos, half, at, block, part, hop, mid, fin, give, got, full, send, recv):
        self.pos, self.half, self.block = pos, half, block
        self.part, self.hop, self.mid, self.fin = part, hop, mid, fin
        self.give, self.got, self.full, self.send, self.recv = give, got, full, send, recv
        self.far, self.above, self.below = (pos + 2) % 4, (pos + 1) % 4, (pos + 3) % 4
        self.first_of = at(self.above, 0)
        self.second_of = at(self.below, 1)
        self.up, self.down = at(self.above, half), at(self.below, half)
        self.up_across, self.down_across = at(self.above, 1 - half), at(self.below, 1 - half)
        self.pair = at(pos, 1 - half)
        self.sent = []

    def peers(self):
        return [self.up, self.down, self.up_across, self.down_across, self.pair]

    def copy(self, src, dst, index, device, landing=None):
        return pltpu.make_async_remote_copy(
            src_ref=src,
            dst_ref=dst,
            send_sem=self.send.at[index],
            recv_sem=self.recv.at[index if landing is None else landing],
            device_id=device,
            device_id_type=MESH,
        )

    def start(self, src, dst, index, device, landing=None):
        copy = self.copy(src, dst, index, device, landing)
        copy.start()
        self.sent.append(copy)
        return copy

    def reduce(self, make, idle=None, between=lambda: None):
        pos, half, part, fin, mid = self.pos, self.half, self.part, self.fin, self.mid
        make(self.far)
        first_up = self.start(part.at[self.far, 0], self.hop.at[0], 0, self.up)
        first_down = self.start(part.at[self.far, 1], self.hop.at[1], 1, self.down)
        between()
        make(self.above)
        direct_up = self.start(part.at[self.above, 1], fin.at[1, 0], 2, self.up)
        between()
        make(self.below)
        direct_down = self.start(part.at[self.below, 0], fin.at[0, 0], 3, self.down)
        between()
        make(pos)
        between()
        first_up.wait_recv()
        mid[0] = (part[self.above, 0].astype(F32) + self.hop[0].astype(F32)).astype(BF16)
        self.start(mid.at[0], fin.at[half, 1], 4, self.first_of, 4 + half)
        between()
        first_down.wait_recv()
        mid[1] = (part[self.below, 1].astype(F32) + self.hop[1].astype(F32)).astype(BF16)
        self.start(mid.at[1], fin.at[half, 1], 5, self.second_of, 4 + half)
        between()
        if idle is not None:
            idle()
        direct_up.wait_recv()
        direct_down.wait_recv()
        self.give[...] = self.near_total(1 - half).astype(BF16)
        last = self.start(self.give, self.got, 6, self.pair)
        mine = self.near_total(half)
        between()
        for plane in (0, 1):
            self.copy(mid.at[0], fin.at[plane, 1], 4, self.first_of, 4 + plane).wait_recv()
        mine = mine + fin[0, 1].astype(F32) + fin[1, 1].astype(F32)
        last.wait_recv()
        return mine + self.got[...].astype(F32)

    def near_total(self, half):
        return self.part[self.pos, half].astype(F32) + self.fin[half, 0].astype(F32)

    def slot(self, chunk, half):
        return self.full.at[pl.ds(pl.multiple_of((chunk * 2 + half) * self.block, self.block), self.block)]

    def open(self):
        own = self.slot(self.pos, self.half)
        self.start(own, own, 8, self.up)
        self.start(own, own, 9, self.down)
        self.start(own, own, 11, self.down_across)
        self.start(own, own, 10, self.up_across)
        self.start(own, own, 7, self.pair)

    def await_slot(self, chunk, half, index):
        slot = self.slot(chunk, half)
        self.copy(slot, slot, index, self.pair).wait_recv()
        return slot

    def pass_on(self):
        early = self.await_slot(self.below, self.half, 8)
        self.start(early, early, 12, self.up)
        late = self.await_slot(self.above, 1 - self.half, 11)
        self.start(late, late, 13, self.down)

    def collect(self, arrived, between=lambda: None):
        half = self.half
        self.await_slot(self.pos, 1 - half, 7)
        arrived(self.pos)
        between()
        self.await_slot(self.above, half, 9)
        arrived(self.above)
        between()
        self.await_slot(self.below, 1 - half, 10)
        arrived(self.below)
        between()
        self.await_slot(self.far, half, 12)
        self.await_slot(self.far, 1 - half, 13)
        arrived(self.far)

    def finish(self):
        for copy in self.sent:
            copy.wait_send()


def kernel(
    ids, tokens, targets, anchor, momentum,
    moment_out, total_out,
    weights, moment, gone, cast, out_box, in_box, twin_out, twin_in,
    inputs, hidden, slope, back, want,
    near_inputs, near_hidden, near_slope, near_back, near_error, relay,
    part, hop, mid, fin, give, got, error,
    part2, hop2, mid2, fin2, give2, got2, total,
    send, recv, send2, recv2, send3, recv3, box_send, box_recv, near_send, near_recv,
    relay_send, relay_recv, twin_send, twin_recv, core_send, core_recv, local,
):
    rep, ten = lax.axis_index("replica"), lax.axis_index("tensor")
    row, side = ten // 2, ten % 2
    low, depth, core = rep // 8, (rep // 2) % 4, rep % 2

    def plane(shift):
        return low * 8 + (depth + shift) % 4 * 2 + core

    def tensor_at(pos, half):
        return (rep, pos * 2 + half)

    def mean_at(pos, half):
        return (half * 8 + pos * 2 + core, ten)

    up2, down2 = (plane(1), ten), (plane(3), ten)
    twin = (low * 8 + depth * 2 + 1 - core, ten)
    after, second = ((rep + 1) % 16, ten), ((rep + 2) % 16, ten)
    relay_end = ((plane(2) + 2) % 16, ten)
    past = (rep + 14) % 16
    relay_start = (past // 8 * 8 + ((past // 2) % 4 + 2) % 4 * 2 + core, ten)

    load = [
        pltpu.make_async_copy(anchor.at[0], weights.at[0], local.at[0]),
        pltpu.make_async_copy(anchor.at[1], weights.at[1], local.at[1]),
        pltpu.make_async_copy(momentum.at[0], moment, local.at[2]),
    ]
    for copy in load:
        copy.start()

    shard_rows = inputs.shape[0] // 8
    mean_ring = Exchange(
        depth, low, mean_at, inputs.shape[1] // 8, part2, hop2, mid2, fin2,
        give2, got2, total.at[core], send2, recv2,
    )
    rings = [
        Exchange(
            row, side, tensor_at, shard_rows, part, hop.at[step], mid, fin.at[step],
            give, got.at[step], error.at[step], send.at[step], recv.at[step],
        )
        for step in range(INNER)
    ]
    near_ring = Exchange(
        row, side, tensor_at, shard_rows, part, None, mid, None,
        give, None, near_error, send3, recv3,
    )
    barrier = pltpu.get_barrier_semaphore()
    peers = rings[0].peers() + mean_ring.peers() + [twin, relay_end, relay_start]
    peers += [((rep + shift) % 16, ten) for shift in (1, 2, 14, 15)]
    for peer in peers:
        pl.semaphore_signal(barrier, inc=1, device_id=peer, device_id_type=MESH)

    rows, width = inputs.shape
    units = hidden.shape[1]
    blocks = 4
    tall = width // blocks
    chunk_rows = rows // 4

    def remote(src, dst, send_sem, recv_sem, device):
        return pltpu.make_async_remote_copy(
            src_ref=src, dst_ref=dst, send_sem=send_sem, recv_sem=recv_sem,
            device_id=device, device_id_type=MESH,
        )

    def chunk_at(chunk):
        return pl.ds(pl.multiple_of(chunk * chunk_rows, chunk_rows), chunk_rows)

    def block_at(j):
        return pl.ds(pl.multiple_of(j * tall, tall), tall)

    def picked(step, chunk, table):
        chosen = ids[step, :, chunk_at(chunk)]
        places = lax.broadcasted_iota(jnp.int32, (rows, chunk_rows), 0)
        mask = jnp.where(chosen == places, 1.0, 0.0).astype(BF16)
        return contract(mask, table[...], 0, 0)

    def fetch(step):
        def some(i, carry):
            inputs[chunk_at(i), :] = picked(step, i, tokens).astype(BF16)
            return carry

        lax.fori_loop(0, 4, some, 0)

    def start_cast(i, carry):
        at = pl.ds(pl.multiple_of(i * 128, 128), 128)
        for m in (0, 1):
            cast[m, at, :] = weights[m, at, :].astype(BF16)
        return carry

    def near_x(i):
        at = chunk_at(i)
        return remote(inputs.at[at], near_inputs.at[at], near_send.at[8 + i], near_recv.at[8 + i], after)

    def near_m(m, j):
        at = block_at(j)
        index = m * blocks + j
        return remote(
            out_box.at[0, m, at], in_box.at[0, m, at], near_send.at[index], near_recv.at[index], after
        )

    def near_shard():
        own = pl.ds(pl.multiple_of(ten * shard_rows, shard_rows), shard_rows)
        return remote(error.at[0, own], near_error.at[own], near_send.at[12], near_recv.at[12], after)

    pieces = [("x", 0, i) for i in range(4)] + [("m", m, j) for m in (1, 0) for j in range(4)]

    def drip():
        if not pieces:
            return
        kind, m, j = pieces.pop(0)
        if kind == "x":
            near_x(j).start()
            return
        if (m, j) == (1, 0):
            load[2].wait()

        def decay(i, carry):
            at = pl.ds(pl.multiple_of(j * tall + i * 64, 64), 64)
            out_box[0, m, at, :] = (inner_beta * moment[m, at, :]).astype(BF16)
            return carry

        lax.fori_loop(0, tall // 64, decay, 0)
        near_m(m, j).start()

    def box(m, j):
        at = block_at(j)
        index = m * blocks + j
        return remote(
            out_box.at[1, m, at], in_box.at[1, m, at], box_send.at[index], box_recv.at[index], second
        )

    def leg(hop_index, j):
        src = out_box.at[1, 1, block_at(j)] if hop_index == 0 else relay.at[hop_index - 1, j]
        dst = in_box.at[1, 1, block_at(j)] if hop_index == 2 else relay.at[hop_index, j]
        return remote(
            src, dst, relay_send.at[hop_index, j], relay_recv.at[hop_index, j],
            relay_end if hop_index == 2 else down2,
        )

    def twin_box(j):
        at = block_at(j)
        return remote(twin_out.at[at], twin_in.at[at], twin_send.at[j], twin_recv.at[j], twin)

    fetch(0)
    load[0].wait()
    load[1].wait()
    lax.fori_loop(0, width // 128, start_cast, 0)
    pl.semaphore_wait(barrier, len(peers))
    drip()

    def one_step(step):
        ring = rings[step]

        def forward(source, at, kept, rise):
            pre = jnp.dot(source[at, :], cast[0], preferred_element_type=F32)
            value, tilt = gelu_pair(pre)
            value = value.astype(BF16)
            kept[at, :] = value
            rise[at, :] = tilt
            return value

        def make(chunk):
            value = forward(inputs, chunk_at(chunk), hidden, slope)
            out = contract(value, cast[1], 1, 1)
            part[chunk] = out.astype(BF16).reshape(2, shard_rows, width)

        def idle():
            want[...] = picked(step, row, targets).reshape(2, shard_rows, width)

        summed = ring.reduce(make, idle, drip if step == 0 else lambda: None)
        own = pl.ds(pl.multiple_of(ten * shard_rows, shard_rows), shard_rows)
        error[step, own, :] = ((summed - want[side]) * (1.0 / rows)).astype(BF16)

        def pull(source, at, rise, result):
            slide = jnp.dot(source[at, :], cast[1], preferred_element_type=F32)
            result[at, :] = (slide * rise[at, :]).astype(BF16)

        def arrived(chunk):
            pull(error.at[step], chunk_at(chunk), slope, back)

        def near_forward(part_of):
            for i in (part_of * 2, part_of * 2 + 1):
                near_x(i).wait_recv()

            def one(i, carry):
                forward(near_inputs, chunk_at(i), near_hidden, near_slope)
                return carry

            lax.fori_loop(part_of * 2, part_of * 2 + 2, one, 0)

        ring.open()
        if step == 0:
            near_shard().start()
            drip()
            near_forward(0)
            drip()
            ring.pass_on()
            near_shard().wait_recv()
            near_ring.open()
            drip()
            ring.collect(arrived, drip)
            while pieces:
                drip()
            near_ring.pass_on()
            near_forward(1)
        else:
            ring.pass_on()
            ring.collect(arrived)

        def update(m, left, right, first, last, ship):
            def one(j, carry):
                at = block_at(j)
                fresh = inner_beta * moment[m, at, :] + contract(left[:, at], right[...], 0, 0)
                moment[m, at, :] = fresh
                moved = fresh if step == 0 else gone[m, at, :] + fresh
                gone[m, at, :] = moved
                if step < 2:
                    kept = weights[m, at, :] - learn_rate * fresh
                    weights[m, at, :] = kept
                if step == 1:
                    out_box[1, m, at, :] = kept.astype(BF16)
                    ship(j).start()
                if step == 2:

                    @pl.when(core == 1 - m)
                    def _():
                        twin_out[at, :] = moved.astype(BF16)
                        twin_box(j).start()

                return carry

            lax.fori_loop(first, last, one, 0)

        def blend(m, at, other):
            mixed = 0.5 * (weights[m, at, :] + other)
            weights[m, at, :] = mixed
            cast[m, at, :] = mixed.astype(BF16)

        if step == 1:
            update(1, error.at[step], hidden, 0, 2, lambda j: leg(0, j))
            update(1, error.at[step], hidden, 2, 4, lambda j: box(1, j))
            update(0, inputs, back, 0, 4, lambda j: box(0, j))
        else:
            update(1, error.at[step], hidden, 0, 4, None)
            update(0, inputs, back, 0, 4, None)
        ring.finish()

        if step == 0:
            for i in range(4):
                near_x(i).wait_send()
            fetch(1)
            near_ring.collect(
                lambda chunk: pull(near_error, chunk_at(chunk), near_slope, near_back)
            )
            for m in (1, 0):
                for j in range(blocks):
                    near_m(m, j).wait_recv()
            for m, left, right in ((1, near_error, near_hidden), (0, near_inputs, near_back)):

                def one(j, carry):
                    at = block_at(j)
                    grad = contract(left[:, at], right[...], 0, 0)
                    began = weights[m, at, :] + learn_rate * moment[m, at, :]
                    near = began - learn_rate * (in_box[0, m, at, :].astype(F32) + grad)
                    blend(m, at, near.astype(BF16).astype(F32))
                    return carry

                lax.fori_loop(0, blocks, one, 0)
            for m in (1, 0):
                for j in range(blocks):
                    near_m(m, j).wait_send()
            near_shard().wait_send()
            near_ring.finish()

        if step == 1:

            def take(m, j, copy):
                copy.wait_recv()
                blend(m, block_at(j), in_box[1, m, block_at(j), :].astype(F32))

            def relay_on(hop_index, j):
                leg(hop_index, j).wait_recv()
                leg(hop_index + 1, j).start()

            fetch(2)
            relay_on(0, 0)
            take(1, 2, box(1, 2))
            relay_on(0, 1)
            take(1, 3, box(1, 3))
            relay_on(1, 0)
            take(0, 0, box(0, 0))
            relay_on(1, 1)
            take(0, 1, box(0, 1))
            take(1, 0, leg(2, 0))
            take(0, 2, box(0, 2))
            take(1, 1, leg(2, 1))
            take(0, 3, box(0, 3))
            for m, j in ((1, 2), (1, 3), (0, 0), (0, 1), (0, 2), (0, 3)):
                box(m, j).wait_send()
            for hop_index in range(3):
                for j in (0, 1):
                    leg(hop_index, j).wait_send()

    for step in range(INNER):
        one_step(step)

    store = pltpu.make_async_copy(moment, moment_out.at[0], local.at[2])
    store.start()

    ring = mean_ring

    def join(chunk):
        at = pl.ds(pl.multiple_of(chunk * tall, tall), tall)
        twin_box(chunk).wait_recv()
        both = gone[core, at, :] + twin_in[at, :].astype(F32)
        part2[chunk] = both.astype(BF16).reshape(2, tall // 2, units)

    summed = ring.reduce(join)
    own = pl.ds(pl.multiple_of((depth * 2 + low) * (width // 8), width // 8), width // 8)
    total[core, own, :] = summed.astype(BF16)

    def across(which, chunk):
        at = pl.ds(pl.multiple_of(chunk * tall, tall), tall)
        return pltpu.make_async_remote_copy(
            src_ref=total.at[which, at],
            dst_ref=total.at[which, at],
            send_sem=core_send.at[chunk],
            recv_sem=core_recv.at[chunk],
            device_id=twin,
            device_id_type=MESH,
        )

    ring.open()
    ring.pass_on()
    ring.collect(lambda chunk: across(core, chunk).start())
    for chunk in range(4):
        across(1 - core, chunk).wait_recv()
    save = pltpu.make_async_copy(total, total_out, local.at[0])
    save.start()
    for chunk in range(4):
        across(core, chunk).wait_send()
        twin_box(chunk).wait_send()
    ring.finish()
    save.wait()
    store.wait()


def body(tokens, targets, row_ids, anchor, momentum, slow):
    rows, width = tokens.shape
    units = anchor.shape[2]
    shard, wide = rows // 8, width // 8
    any_spec = pl.BlockSpec(memory_space=pl.ANY)
    vmem_spec = pl.BlockSpec(memory_space=pltpu.VMEM)
    dma = pltpu.SemaphoreType.DMA
    ids = row_ids.reshape(INNER, 1, rows)
    moment, total = pl.pallas_call(
        kernel,
        name="outer_round",
        out_shape=(
            jax.ShapeDtypeStruct(momentum.shape, F32),
            jax.ShapeDtypeStruct(anchor.shape, BF16),
        ),
        in_specs=[vmem_spec, vmem_spec, vmem_spec, any_spec, any_spec],
        out_specs=(any_spec, any_spec),
        scratch_shapes=[
            pltpu.VMEM((2, width, units), F32),
            pltpu.VMEM((2, width, units), F32),
            pltpu.VMEM((2, width, units), F32),
            pltpu.VMEM((2, width, units), BF16),
            pltpu.VMEM((2, 2, width, units), BF16),
            pltpu.VMEM((2, 2, width, units), BF16),
            pltpu.VMEM((width, units), BF16),
            pltpu.VMEM((width, units), BF16),
            pltpu.VMEM((rows, width), BF16),
            pltpu.VMEM((rows, units), BF16),
            pltpu.VMEM((rows, units), F32),
            pltpu.VMEM((rows, units), BF16),
            pltpu.VMEM((2, shard, width), F32),
            pltpu.VMEM((rows, width), BF16),
            pltpu.VMEM((rows, units), BF16),
            pltpu.VMEM((rows, units), F32),
            pltpu.VMEM((rows, units), BF16),
            pltpu.VMEM((rows, width), BF16),
            pltpu.VMEM((2, 2, width // 4, units), BF16),
            pltpu.VMEM((4, 2, shard, width), BF16),
            pltpu.VMEM((INNER, 2, shard, width), BF16),
            pltpu.VMEM((2, shard, width), BF16),
            pltpu.VMEM((INNER, 2, 2, shard, width), BF16),
            pltpu.VMEM((shard, width), BF16),
            pltpu.VMEM((INNER, shard, width), BF16),
            pltpu.VMEM((INNER, rows, width), BF16),
            pltpu.VMEM((4, 2, wide, units), BF16),
            pltpu.VMEM((2, wide, units), BF16),
            pltpu.VMEM((2, wide, units), BF16),
            pltpu.VMEM((2, 2, wide, units), BF16),
            pltpu.VMEM((wide, units), BF16),
            pltpu.VMEM((wide, units), BF16),
            pltpu.VMEM((2, width, units), BF16),
            dma((INNER, 14)),
            dma((INNER, 14)),
            dma((14,)),
            dma((14,)),
            dma((14,)),
            dma((14,)),
            dma((8,)),
            dma((8,)),
            dma((13,)),
            dma((13,)),
            dma((3, 2)),
            dma((3, 2)),
            dma((4,)),
            dma((4,)),
            dma((4,)),
            dma((4,)),
            dma((3,)),
        ],
        compiler_params=pltpu.CompilerParams(
            collective_id=0, has_side_effects=True, vmem_limit_bytes=60 * 1024 * 1024
        ),
    )(ids, tokens, targets, anchor, momentum)
    mean = total.astype(F32) * (1.0 / lax.axis_size("replica"))
    slow_new = slow_beta * slow + mean
    anchor_new = anchor - learn_rate * slow_new
    return (anchor_new, slow_new, moment)


def solution(mesh):
    return jax.shard_map(
        body,
        mesh=mesh,
        in_specs=(
            P("replica", None),
            P("replica", None),
            P("replica", None, None),
            P(None, None, "tensor"),
            P("replica", None, None, "tensor"),
            P(None, None, "tensor"),
        ),
        out_specs=(
            P(None, None, "tensor"),
            P(None, None, "tensor"),
            P("replica", None, None, "tensor"),
        ),
        check_vma=False,
    )
```

```python
import functools

import jax
import jax.numpy as jnp
from jax import lax
from jax.experimental import pallas as pl
from jax.experimental.pallas import tpu as pltpu
from jax.sharding import PartitionSpec as P

INNER = 3
learn_rate = 0.02
inner_beta = 0.9
slow_beta = 0.5

F32 = jnp.float32
BF16 = jnp.bfloat16
MESH = pl.DeviceIdType.MESH


def gelu_pair(pre):
    coeff = 0.7978845608028654
    square = pre * pre
    tanh_val = jnp.tanh(coeff * (pre + 0.044715 * pre * square))
    upper = 0.5 * (1.0 + tanh_val)
    value = pre * upper
    slope = upper + 0.5 * pre * (1.0 - tanh_val * tanh_val) * coeff * (
        1.0 + 3.0 * 0.044715 * square
    )
    return (value, slope)


def contract(a, b, dim_a, dim_b):
    return lax.dot_general(a, b, (((dim_a,), (dim_b,)), ((), ())), preferred_element_type=F32)


class Exchange:
    def __init__(self, pos, half, at, block, part, hop, mid, fin, give, got, full, send, recv):
        self.pos, self.half, self.block = pos, half, block
        self.part, self.hop, self.mid, self.fin = part, hop, mid, fin
        self.give, self.got, self.full, self.send, self.recv = give, got, full, send, recv
        self.far, self.above, self.below = (pos + 2) % 4, (pos + 1) % 4, (pos + 3) % 4
        self.first_of = at(self.above, 0)
        self.second_of = at(self.below, 1)
        self.up, self.down = at(self.above, half), at(self.below, half)
        self.up_across, self.down_across = at(self.above, 1 - half), at(self.below, 1 - half)
        self.pair = at(pos, 1 - half)
        self.sent = []

    def peers(self):
        return [self.up, self.down, self.up_across, self.down_across, self.pair]

    def copy(self, src, dst, index, device, landing=None):
        return pltpu.make_async_remote_copy(
            src_ref=src,
            dst_ref=dst,
            send_sem=self.send.at[index],
            recv_sem=self.recv.at[index if landing is None else landing],
            device_id=device,
            device_id_type=MESH,
        )

    def start(self, src, dst, index, device, landing=None):
        copy = self.copy(src, dst, index, device, landing)
        copy.start()
        self.sent.append(copy)
        return copy

    def reduce(self, make, idle=None, between=lambda: None):
        pos, half, part, fin, mid = self.pos, self.half, self.part, self.fin, self.mid
        make(self.far)
        first_up = self.start(part.at[self.far, 0], self.hop.at[0], 0, self.up)
        first_down = self.start(part.at[self.far, 1], self.hop.at[1], 1, self.down)
        between()
        make(self.above)
        direct_up = self.start(part.at[self.above, 1], fin.at[1, 0], 2, self.up)
        between()
        make(self.below)
        direct_down = self.start(part.at[self.below, 0], fin.at[0, 0], 3, self.down)
        between()
        make(pos)
        between()
        first_up.wait_recv()
        mid[0] = (part[self.above, 0].astype(F32) + self.hop[0].astype(F32)).astype(BF16)
        self.start(mid.at[0], fin.at[half, 1], 4, self.first_of, 4 + half)
        between()
        first_down.wait_recv()
        mid[1] = (part[self.below, 1].astype(F32) + self.hop[1].astype(F32)).astype(BF16)
        self.start(mid.at[1], fin.at[half, 1], 5, self.second_of, 4 + half)
        if idle is not None:
            idle()
        direct_up.wait_recv()
        direct_down.wait_recv()
        self.give[...] = self.near_total(1 - half).astype(BF16)
        last = self.start(self.give, self.got, 6, self.pair)
        mine = self.near_total(half)
        for plane in (0, 1):
            self.copy(mid.at[0], fin.at[plane, 1], 4, self.first_of, 4 + plane).wait_recv()
        mine = mine + fin[0, 1].astype(F32) + fin[1, 1].astype(F32)
        last.wait_recv()
        return mine + self.got[...].astype(F32)

    def near_total(self, half):
        return self.part[self.pos, half].astype(F32) + self.fin[half, 0].astype(F32)

    def slot(self, chunk, half):
        return self.full.at[pl.ds(pl.multiple_of((chunk * 2 + half) * self.block, self.block), self.block)]

    def open(self):
        own = self.slot(self.pos, self.half)
        self.start(own, own, 8, self.up)
        self.start(own, own, 9, self.down)
        self.start(own, own, 11, self.down_across)
        self.start(own, own, 10, self.up_across)
        self.start(own, own, 7, self.pair)

    def await_slot(self, chunk, half, index):
        slot = self.slot(chunk, half)
        self.copy(slot, slot, index, self.pair).wait_recv()
        return slot

    def pass_on(self):
        early = self.await_slot(self.below, self.half, 8)
        self.start(early, early, 12, self.up)
        late = self.await_slot(self.above, 1 - self.half, 11)
        self.start(late, late, 13, self.down)

    def collect(self, arrived, between=lambda: None):
        half = self.half
        self.await_slot(self.pos, 1 - half, 7)
        arrived(self.pos)
        between()
        self.await_slot(self.above, half, 9)
        arrived(self.above)
        between()
        self.await_slot(self.below, 1 - half, 10)
        arrived(self.below)
        between()
        self.await_slot(self.far, half, 12)
        self.await_slot(self.far, 1 - half, 13)
        arrived(self.far)

    def finish(self):
        for copy in self.sent:
            copy.wait_send()

    def finish_gather(self):
        for index in range(7, 14):
            slot = self.slot(self.pos, self.half)
            self.copy(slot, slot, index, self.pair).wait_send()


def kernel(
    ids, tokens, targets, anchor, momentum,
    moment_out, total_out,
    weights, moment, gone, cast, out_box, in_box, twin_out, twin_in,
    inputs, hidden, slope, back, want,
    near_inputs, near_hidden, near_slope, near_back, near_error, relay, carried,
    part, hop, mid, fin, give, got, error,
    part2, hop2, mid2, fin2, give2, got2, total,
    send, recv, send2, recv2, send3, recv3, box_send, box_recv, near_send, near_recv, turn_send, turn_recv,
    relay_send, relay_recv, twin_send, twin_recv, core_send, core_recv, local,
):
    rep, ten = lax.axis_index("replica"), lax.axis_index("tensor")
    row, side = ten // 2, ten % 2
    low, depth, core = rep // 8, (rep // 2) % 4, rep % 2

    def plane(shift):
        return low * 8 + (depth + shift) % 4 * 2 + core

    def tensor_at(pos, half):
        return (rep, pos * 2 + half)

    def mean_at(pos, half):
        return (half * 8 + pos * 2 + core, ten)

    up2, down2 = (plane(1), ten), (plane(3), ten)
    twin = (low * 8 + depth * 2 + 1 - core, ten)
    after, second = ((rep + 1) % 16, ten), ((rep + 2) % 16, ten)
    relay_end = ((plane(2) + 2) % 16, ten)
    past = (rep + 14) % 16
    ships = (depth != 3) | (core != 1)
    hears = (depth != 0) | (core != 0)
    turner = (low * 8 + (depth + 1) % 4 * 2 + 1 - core, ten)
    turned = (low * 8 + (depth + 3) % 4 * 2 + 1 - core, ten)
    beside = ((1 - low) * 8 + depth * 2 + core, ten)
    relay_start = (past // 8 * 8 + ((past // 2) % 4 + 2) % 4 * 2 + core, ten)

    load = [
        pltpu.make_async_copy(anchor.at[0], weights.at[0], local.at[0]),
        pltpu.make_async_copy(anchor.at[1], weights.at[1], local.at[1]),
        pltpu.make_async_copy(momentum.at[0], moment, local.at[2]),
    ]
    for copy in load:
        copy.start()

    shard_rows = inputs.shape[0] // 8
    mean_ring = Exchange(
        depth, low, mean_at, inputs.shape[1] // 8, part2, hop2, mid2, fin2,
        give2, got2, total.at[core], send2, recv2,
    )
    rings = [
        Exchange(
            row, side, tensor_at, shard_rows, part, hop.at[step], mid, fin.at[step],
            give, got.at[step], error.at[step], send.at[step], recv.at[step],
        )
        for step in range(INNER)
    ]
    near_ring = Exchange(
        row, side, tensor_at, shard_rows, part, None, mid, None,
        give, None, near_error, send3, recv3,
    )
    barrier = pltpu.get_barrier_semaphore()
    peers = rings[0].peers() + mean_ring.peers() + [twin, relay_end, relay_start, turner, turned]
    peers += [((rep + shift) % 16, ten) for shift in (1, 2, 14, 15)]
    for peer in peers:
        pl.semaphore_signal(barrier, inc=1, device_id=peer, device_id_type=MESH)

    rows, width = inputs.shape
    units = hidden.shape[1]
    blocks = 4
    tall = width // blocks
    chunk_rows = rows // 4

    def remote(src, dst, send_sem, recv_sem, device):
        return pltpu.make_async_remote_copy(
            src_ref=src, dst_ref=dst, send_sem=send_sem, recv_sem=recv_sem,
            device_id=device, device_id_type=MESH,
        )

    def chunk_at(chunk):
        return pl.ds(pl.multiple_of(chunk * chunk_rows, chunk_rows), chunk_rows)

    def block_at(j):
        return pl.ds(pl.multiple_of(j * tall, tall), tall)

    def picked(step, chunk, table):
        chosen = ids[step, :, chunk_at(chunk)]
        places = lax.broadcasted_iota(jnp.int32, (rows, chunk_rows), 0)
        mask = jnp.where(chosen == places, 1.0, 0.0).astype(BF16)
        return contract(mask, table[...], 0, 0)

    def fetch(step):
        def some(i, carry):
            inputs[chunk_at(i), :] = picked(step, i, tokens).astype(BF16)
            return carry

        lax.fori_loop(0, 4, some, 0)

    def start_cast(i, carry):
        at = pl.ds(pl.multiple_of(i * 128, 128), 128)
        for m in (0, 1):
            cast[m, at, :] = weights[m, at, :].astype(BF16)
        return carry

    def near_x(i):
        at = chunk_at(i)
        return remote(inputs.at[at], near_inputs.at[at], near_send.at[8 + i], near_recv.at[8 + i], after)

    def near_m(m, j):
        at = block_at(j)
        index = m * blocks + j
        return remote(
            out_box.at[0, m, at], in_box.at[0, m, at], near_send.at[index], near_recv.at[index], after
        )

    def near_shard():
        own = pl.ds(pl.multiple_of(ten * shard_rows, shard_rows), shard_rows)
        return remote(error.at[0, own], near_error.at[own], near_send.at[12], near_recv.at[12], after)

    pieces = [("x", 0, i) for i in range(4)] + [("m", m, j) for m in (1, 0) for j in range(4)]

    def drip():
        if not pieces:
            return
        kind, m, j = pieces.pop(0)
        if (kind, m, j) == ("m", 1, 0):
            load[2].wait()

        @pl.when(ships)
        def _():
            if kind == "x":
                near_x(j).start()
                return

            def decay(i, carry):
                at = pl.ds(pl.multiple_of(j * tall + i * 64, 64), 64)
                out_box[0, m, at, :] = (inner_beta * moment[m, at, :]).astype(BF16)
                return carry

            lax.fori_loop(0, tall // 64, decay, 0)
            near_m(m, j).start()

    def straight(m, j):
        at = block_at(j)
        index = m * blocks + j
        return remote(
            out_box.at[0, m, at], in_box.at[0, m, at], turn_send.at[index], turn_recv.at[index], after
        )

    def turn_first(m, j):
        index, place = m * blocks + j, m * 2 + j // 2
        return remote(
            out_box.at[0, m, block_at(j)], carried.at[place],
            turn_send.at[index], turn_recv.at[8 + place], turner,
        )

    def turn_second(m, j):
        index, place = m * blocks + j, m * 2 + j // 2
        return remote(
            carried.at[place], in_box.at[0, m, block_at(j)],
            turn_send.at[8 + place], turn_recv.at[index], beside,
        )

    def box(m, j):
        at = block_at(j)
        index = m * blocks + j
        return remote(
            out_box.at[1, m, at], in_box.at[1, m, at], box_send.at[index], box_recv.at[index], second
        )

    def leg(hop_index, j):
        src = out_box.at[1, 1, block_at(j)] if hop_index == 0 else relay.at[hop_index - 1, j]
        dst = in_box.at[1, 1, block_at(j)] if hop_index == 2 else relay.at[hop_index, j]
        return remote(
            src, dst, relay_send.at[hop_index, j], relay_recv.at[hop_index, j],
            relay_end if hop_index == 2 else down2,
        )

    def twin_box(j):
        at = block_at(j)
        return remote(twin_out.at[at], twin_in.at[at], twin_send.at[j], twin_recv.at[j], twin)

    fetch(0)
    load[0].wait()
    load[1].wait()
    lax.fori_loop(0, width // 128, start_cast, 0)
    pl.semaphore_wait(barrier, len(peers))
    drip()

    def one_step(step):
        ring = rings[step]

        def forward(source, at, kept, rise):
            pre = jnp.dot(source[at, :], cast[0], preferred_element_type=F32)
            value, tilt = gelu_pair(pre)
            value = value.astype(BF16)
            kept[at, :] = value
            rise[at, :] = tilt
            return value

        def make(chunk):
            value = forward(inputs, chunk_at(chunk), hidden, slope)
            out = contract(value, cast[1], 1, 1)
            part[chunk] = out.astype(BF16).reshape(2, shard_rows, width)

        def idle():
            want[...] = picked(step, row, targets).reshape(2, shard_rows, width)

        summed = ring.reduce(make, idle, drip if step == 0 else lambda: None)
        own = pl.ds(pl.multiple_of(ten * shard_rows, shard_rows), shard_rows)
        error[step, own, :] = ((summed - want[side]) * (1.0 / rows)).astype(BF16)

        def pull(source, at, rise, result):
            slide = jnp.dot(source[at, :], cast[1], preferred_element_type=F32)
            result[at, :] = (slide * rise[at, :]).astype(BF16)

        def arrived(chunk):
            pull(error.at[step], chunk_at(chunk), slope, back)

        def near_forward(part_of):
            for i in (part_of * 2, part_of * 2 + 1):
                near_x(i).wait_recv()

            def one(i, carry):
                forward(near_inputs, chunk_at(i), near_hidden, near_slope)
                return carry

            lax.fori_loop(part_of * 2, part_of * 2 + 2, one, 0)

        ring.open()
        if step == 0:

            @pl.when(ships)
            def _():
                near_shard().start()

            drip()

            @pl.when(hears)
            def _():
                near_forward(0)

            drip()
            ring.pass_on()

            @pl.when(hears)
            def _():
                near_shard().wait_recv()
                near_ring.open()

            drip()
            ring.collect(arrived, drip)
            while pieces:
                drip()

            @pl.when(hears)
            def _():
                near_ring.pass_on()
                near_forward(1)

        else:
            ring.pass_on()
            ring.collect(arrived)

        def update(m, left, right, first, last, ship):
            def one(j, carry):
                at = block_at(j)
                fresh = inner_beta * moment[m, at, :] + contract(left[:, at], right[...], 0, 0)
                moment[m, at, :] = fresh
                moved = fresh if step == 0 else gone[m, at, :] + fresh
                gone[m, at, :] = moved
                if step < 2:
                    kept = weights[m, at, :] - learn_rate * fresh
                    weights[m, at, :] = kept
                if step == 0:

                    @pl.when(jnp.logical_not(ships))
                    def _():
                        out_box[0, m, at, :] = kept.astype(BF16)

                        @pl.when(j % 2 == 0)
                        def _():
                            straight(m, j).start()

                        @pl.when(j % 2 == 1)
                        def _():
                            turn_first(m, j).start()

                if step == 1:
                    out_box[1, m, at, :] = kept.astype(BF16)
                    ship(j).start()
                if step == 2:

                    @pl.when(core == 1 - m)
                    def _():
                        twin_out[at, :] = moved.astype(BF16)
                        twin_box(j).start()

                return carry

            lax.fori_loop(first, last, one, 0)

        def blend(m, at, other):
            mixed = 0.5 * (weights[m, at, :] + other)
            weights[m, at, :] = mixed
            cast[m, at, :] = mixed.astype(BF16)

        if step == 1:
            update(1, error.at[step], hidden, 0, 2, lambda j: leg(0, j))
            update(1, error.at[step], hidden, 2, 4, lambda j: box(1, j))
            update(0, inputs, back, 0, 4, lambda j: box(0, j))
        elif step == 0:
            update(1, error.at[step], hidden, 0, 4, None)
            update(0, inputs, back, 0, 4, None)
        else:
            @pl.when(core == 0)
            def _():
                update(1, error.at[step], hidden, 0, 4, None)
                update(0, inputs, back, 0, 4, None)

            @pl.when(core == 1)
            def _():
                update(0, inputs, back, 0, 4, None)
                update(1, error.at[step], hidden, 0, 4, None)

        ring.finish()

        if step == 0:

            @pl.when(ships)
            def _():
                for i in range(4):
                    near_x(i).wait_send()

            fetch(1)

            @pl.when(hears)
            def _():
                near_ring.collect(
                    lambda chunk: pull(near_error, chunk_at(chunk), near_slope, near_back)
                )
                for m in (1, 0):
                    for j in range(blocks):
                        near_m(m, j).wait_recv()
                for m, left, right in ((1, near_error, near_hidden), (0, near_inputs, near_back)):

                    def one(j, carry):
                        at = block_at(j)
                        grad = contract(left[:, at], right[...], 0, 0)
                        began = weights[m, at, :] + learn_rate * moment[m, at, :]
                        near = began - learn_rate * (in_box[0, m, at, :].astype(F32) + grad)
                        blend(m, at, near.astype(BF16).astype(F32))
                        return carry

                    lax.fori_loop(0, blocks, one, 0)
                near_ring.finish_gather()

            @pl.when(jnp.logical_not(hears))
            def _():
                def pass_turn(m, j):
                    turn_first(m, j).wait_recv()
                    turn_second(m, j).start()

                def take_turn(m, j):
                    straight(m, j).wait_recv()
                    blend(m, block_at(j), in_box[0, m, block_at(j), :].astype(F32))

                pass_turn(1, 1)
                take_turn(1, 0)
                pass_turn(1, 3)
                take_turn(1, 2)
                take_turn(1, 1)
                pass_turn(0, 1)
                take_turn(0, 0)
                take_turn(1, 3)
                pass_turn(0, 3)
                take_turn(0, 2)
                take_turn(0, 1)
                take_turn(0, 3)
                for m in (1, 0):
                    for j in (1, 3):
                        turn_second(m, j).wait_send()

            @pl.when(ships)
            def _():
                for m in (1, 0):
                    for j in range(blocks):
                        near_m(m, j).wait_send()
                near_shard().wait_send()

            @pl.when(jnp.logical_not(ships))
            def _():
                for m in (1, 0):
                    for j in range(blocks):
                        straight(m, j).wait_send()

        if step == 1:

            def take(m, j, copy):
                copy.wait_recv()
                blend(m, block_at(j), in_box[1, m, block_at(j), :].astype(F32))

            def relay_on(hop_index, j):
                leg(hop_index, j).wait_recv()
                leg(hop_index + 1, j).start()

            fetch(2)
            relay_on(0, 0)
            take(1, 2, box(1, 2))
            relay_on(0, 1)
            take(1, 3, box(1, 3))
            relay_on(1, 0)
            take(0, 0, box(0, 0))
            relay_on(1, 1)
            take(0, 1, box(0, 1))
            take(1, 0, leg(2, 0))
            take(0, 2, box(0, 2))
            take(1, 1, leg(2, 1))
            take(0, 3, box(0, 3))
            for m, j in ((1, 2), (1, 3), (0, 0), (0, 1), (0, 2), (0, 3)):
                box(m, j).wait_send()
            for hop_index in range(3):
                for j in (0, 1):
                    leg(hop_index, j).wait_send()

    for step in range(INNER):
        one_step(step)

    store = pltpu.make_async_copy(moment, moment_out.at[0], local.at[2])
    store.start()

    ring = mean_ring

    def join(chunk):
        at = pl.ds(pl.multiple_of(chunk * tall, tall), tall)
        twin_box(chunk).wait_recv()
        both = gone[core, at, :] + twin_in[at, :].astype(F32)
        part2[chunk] = both.astype(BF16).reshape(2, tall // 2, units)

    summed = ring.reduce(join)
    own = pl.ds(pl.multiple_of((depth * 2 + low) * (width // 8), width // 8), width // 8)
    total[core, own, :] = summed.astype(BF16)

    def across(which, chunk):
        at = pl.ds(pl.multiple_of(chunk * tall, tall), tall)
        return pltpu.make_async_remote_copy(
            src_ref=total.at[which, at],
            dst_ref=total.at[which, at],
            send_sem=core_send.at[chunk],
            recv_sem=core_recv.at[chunk],
            device_id=twin,
            device_id_type=MESH,
        )

    ring.open()
    ring.pass_on()
    ring.collect(lambda chunk: across(core, chunk).start())
    for chunk in range(4):
        across(1 - core, chunk).wait_recv()
    save = pltpu.make_async_copy(total, total_out, local.at[0])
    save.start()
    for chunk in range(4):
        across(core, chunk).wait_send()
        twin_box(chunk).wait_send()
    ring.finish()
    save.wait()
    store.wait()


def body(tokens, targets, row_ids, anchor, momentum, slow):
    rows, width = tokens.shape
    units = anchor.shape[2]
    shard, wide = rows // 8, width // 8
    any_spec = pl.BlockSpec(memory_space=pl.ANY)
    vmem_spec = pl.BlockSpec(memory_space=pltpu.VMEM)
    dma = pltpu.SemaphoreType.DMA
    ids = row_ids.reshape(INNER, 1, rows)
    moment, total = pl.pallas_call(
        kernel,
        name="outer_round",
        out_shape=(
            jax.ShapeDtypeStruct(momentum.shape, F32),
            jax.ShapeDtypeStruct(anchor.shape, BF16),
        ),
        in_specs=[vmem_spec, vmem_spec, vmem_spec, any_spec, any_spec],
        out_specs=(any_spec, any_spec),
        scratch_shapes=[
            pltpu.VMEM((2, width, units), F32),
            pltpu.VMEM((2, width, units), F32),
            pltpu.VMEM((2, width, units), F32),
            pltpu.VMEM((2, width, units), BF16),
            pltpu.VMEM((2, 2, width, units), BF16),
            pltpu.VMEM((2, 2, width, units), BF16),
            pltpu.VMEM((width, units), BF16),
            pltpu.VMEM((width, units), BF16),
            pltpu.VMEM((rows, width), BF16),
            pltpu.VMEM((rows, units), BF16),
            pltpu.VMEM((rows, units), F32),
            pltpu.VMEM((rows, units), BF16),
            pltpu.VMEM((2, shard, width), F32),
            pltpu.VMEM((rows, width), BF16),
            pltpu.VMEM((rows, units), BF16),
            pltpu.VMEM((rows, units), F32),
            pltpu.VMEM((rows, units), BF16),
            pltpu.VMEM((rows, width), BF16),
            pltpu.VMEM((2, 2, width // 4, units), BF16),
            pltpu.VMEM((4, width // 4, units), BF16),
            pltpu.VMEM((4, 2, shard, width), BF16),
            pltpu.VMEM((INNER, 2, shard, width), BF16),
            pltpu.VMEM((2, shard, width), BF16),
            pltpu.VMEM((INNER, 2, 2, shard, width), BF16),
            pltpu.VMEM((shard, width), BF16),
            pltpu.VMEM((INNER, shard, width), BF16),
            pltpu.VMEM((INNER, rows, width), BF16),
            pltpu.VMEM((4, 2, wide, units), BF16),
            pltpu.VMEM((2, wide, units), BF16),
            pltpu.VMEM((2, wide, units), BF16),
            pltpu.VMEM((2, 2, wide, units), BF16),
            pltpu.VMEM((wide, units), BF16),
            pltpu.VMEM((wide, units), BF16),
            pltpu.VMEM((2, width, units), BF16),
            dma((INNER, 14)),
            dma((INNER, 14)),
            dma((14,)),
            dma((14,)),
            dma((14,)),
            dma((14,)),
            dma((8,)),
            dma((8,)),
            dma((13,)),
            dma((13,)),
            dma((12,)),
            dma((12,)),
            dma((3, 2)),
            dma((3, 2)),
            dma((4,)),
            dma((4,)),
            dma((4,)),
            dma((4,)),
            dma((3,)),
        ],
        compiler_params=pltpu.CompilerParams(
            collective_id=0, has_side_effects=True, vmem_limit_bytes=46 * 1024 * 1024
        ),
    )(ids, tokens, targets, anchor, momentum)
    mean = total.astype(F32) * (1.0 / lax.axis_size("replica"))
    slow_new = slow_beta * slow + mean
    anchor_new = anchor - learn_rate * slow_new
    return (anchor_new, slow_new, moment)


def solution(mesh):
    return jax.shard_map(
        body,
        mesh=mesh,
        in_specs=(
            P("replica", None),
            P("replica", None),
            P("replica", None, None),
            P(None, None, "tensor"),
            P("replica", None, None, "tensor"),
            P(None, None, "tensor"),
        ),
        out_specs=(
            P(None, None, "tensor"),
            P(None, None, "tensor"),
            P("replica", None, None, "tensor"),
        ),
        check_vma=False,
    )
```

```python
import functools

import jax
import jax.numpy as jnp
from jax import lax
from jax.experimental import pallas as pl
from jax.experimental.pallas import tpu as pltpu
from jax.sharding import PartitionSpec as P

INNER = 3
learn_rate = 0.02
inner_beta = 0.9
slow_beta = 0.5

F32 = jnp.float32
BF16 = jnp.bfloat16
MESH = pl.DeviceIdType.MESH


def gelu_pair(pre):
    coeff = 0.7978845608028654
    square = pre * pre
    tanh_val = jnp.tanh(coeff * (pre + 0.044715 * pre * square))
    upper = 0.5 * (1.0 + tanh_val)
    value = pre * upper
    slope = upper + 0.5 * pre * (1.0 - tanh_val * tanh_val) * coeff * (
        1.0 + 3.0 * 0.044715 * square
    )
    return (value, slope)


def contract(a, b, dim_a, dim_b):
    return lax.dot_general(a, b, (((dim_a,), (dim_b,)), ((), ())), preferred_element_type=F32)


class Exchange:
    def __init__(self, pos, half, at, block, part, hop, mid, fin, give, got, full, send, recv):
        self.pos, self.half, self.block = pos, half, block
        self.part, self.hop, self.mid, self.fin = part, hop, mid, fin
        self.give, self.got, self.full, self.send, self.recv = give, got, full, send, recv
        self.far, self.above, self.below = (pos + 2) % 4, (pos + 1) % 4, (pos + 3) % 4
        self.first_of = at(self.above, 0)
        self.second_of = at(self.below, 1)
        self.up, self.down = at(self.above, half), at(self.below, half)
        self.up_across, self.down_across = at(self.above, 1 - half), at(self.below, 1 - half)
        self.pair = at(pos, 1 - half)
        self.sent = []

    def peers(self):
        return [self.up, self.down, self.up_across, self.down_across, self.pair]

    def copy(self, src, dst, index, device, landing=None):
        return pltpu.make_async_remote_copy(
            src_ref=src,
            dst_ref=dst,
            send_sem=self.send.at[index],
            recv_sem=self.recv.at[index if landing is None else landing],
            device_id=device,
            device_id_type=MESH,
        )

    def start(self, src, dst, index, device, landing=None):
        copy = self.copy(src, dst, index, device, landing)
        copy.start()
        self.sent.append(copy)
        return copy

    def reduce(self, make, idle=None, between=lambda: None):
        pos, half, part, fin, mid = self.pos, self.half, self.part, self.fin, self.mid
        make(self.far)
        first_up = self.start(part.at[self.far, 0], self.hop.at[0], 0, self.up)
        first_down = self.start(part.at[self.far, 1], self.hop.at[1], 1, self.down)
        between()
        make(self.above)
        direct_up = self.start(part.at[self.above, 1], fin.at[1, 0], 2, self.up)
        between()
        make(self.below)
        direct_down = self.start(part.at[self.below, 0], fin.at[0, 0], 3, self.down)
        between()
        make(pos)
        between()
        first_up.wait_recv()
        mid[0] = (part[self.above, 0].astype(F32) + self.hop[0].astype(F32)).astype(BF16)
        self.start(mid.at[0], fin.at[half, 1], 4, self.first_of, 4 + half)
        first_down.wait_recv()
        mid[1] = (part[self.below, 1].astype(F32) + self.hop[1].astype(F32)).astype(BF16)
        self.start(mid.at[1], fin.at[half, 1], 5, self.second_of, 4 + half)
        if idle is not None:
            idle()
        direct_up.wait_recv()
        direct_down.wait_recv()
        self.give[...] = self.near_total(1 - half).astype(BF16)
        last = self.start(self.give, self.got, 6, self.pair)
        mine = self.near_total(half)
        for plane in (0, 1):
            self.copy(mid.at[0], fin.at[plane, 1], 4, self.first_of, 4 + plane).wait_recv()
        mine = mine + fin[0, 1].astype(F32) + fin[1, 1].astype(F32)
        last.wait_recv()
        return mine + self.got[...].astype(F32)

    def near_total(self, half):
        return self.part[self.pos, half].astype(F32) + self.fin[half, 0].astype(F32)

    def slot(self, chunk, half):
        return self.full.at[pl.ds(pl.multiple_of((chunk * 2 + half) * self.block, self.block), self.block)]

    def open(self):
        own = self.slot(self.pos, self.half)
        self.start(own, own, 8, self.up)
        self.start(own, own, 9, self.down)
        self.start(own, own, 11, self.down_across)
        self.start(own, own, 10, self.up_across)
        self.start(own, own, 7, self.pair)

    def await_slot(self, chunk, half, index):
        slot = self.slot(chunk, half)
        self.copy(slot, slot, index, self.pair).wait_recv()
        return slot

    def pass_on(self):
        early = self.await_slot(self.below, self.half, 8)
        self.start(early, early, 12, self.up)
        late = self.await_slot(self.above, 1 - self.half, 11)
        self.start(late, late, 13, self.down)

    def collect(self, arrived, between=lambda: None):
        half = self.half
        self.await_slot(self.pos, 1 - half, 7)
        arrived(self.pos)
        between()
        self.await_slot(self.above, half, 9)
        arrived(self.above)
        between()
        self.await_slot(self.below, 1 - half, 10)
        arrived(self.below)
        between()
        self.await_slot(self.far, half, 12)
        self.await_slot(self.far, 1 - half, 13)
        arrived(self.far)

    def finish(self):
        for copy in self.sent:
            copy.wait_send()

    def finish_gather(self):
        for index in range(7, 14):
            slot = self.slot(self.pos, self.half)
            self.copy(slot, slot, index, self.pair).wait_send()


def kernel(
    ids_far, tokens_far, targets_far, anchor, momentum,
    moment_out, total_out,
    ids, tokens, targets, weights, moment, gone, cast, out_box, in_box, twin_out, twin_in,
    inputs, hidden, slope, back, want,
    near_inputs, near_hidden, near_slope, near_back, near_error, relay, carried,
    part, hop, mid, fin, give, got, error,
    part2, hop2, mid2, fin2, give2, got2, total,
    send, recv, send2, recv2, send3, recv3, box_send, box_recv, near_send, near_recv, turn_send, turn_recv,
    relay_send, relay_recv, twin_send, twin_recv, core_send, core_recv, local,
):
    rep, ten = lax.axis_index("replica"), lax.axis_index("tensor")
    row, side = ten // 2, ten % 2
    low, depth, core = rep // 8, (rep // 2) % 4, rep % 2

    def plane(shift):
        return low * 8 + (depth + shift) % 4 * 2 + core

    def tensor_at(pos, half):
        return (rep, pos * 2 + half)

    def mean_at(pos, half):
        return (half * 8 + pos * 2 + core, ten)

    up2, down2 = (plane(1), ten), (plane(3), ten)
    twin = (low * 8 + depth * 2 + 1 - core, ten)
    after, second = ((rep + 1) % 16, ten), ((rep + 2) % 16, ten)
    relay_end = ((plane(2) + 2) % 16, ten)
    past = (rep + 14) % 16
    ships = (depth != 3) | (core != 1)
    hears = (depth != 0) | (core != 0)
    turner = (low * 8 + (depth + 1) % 4 * 2 + 1 - core, ten)
    turned = (low * 8 + (depth + 3) % 4 * 2 + 1 - core, ten)
    beside = ((1 - low) * 8 + depth * 2 + core, ten)
    relay_start = (past // 8 * 8 + ((past // 2) % 4 + 2) % 4 * 2 + core, ten)

    load = [
        pltpu.make_async_copy(anchor.at[0], weights.at[0], local.at[0]),
        pltpu.make_async_copy(anchor.at[1], weights.at[1], local.at[1]),
        pltpu.make_async_copy(momentum.at[0], moment, local.at[2]),
        pltpu.make_async_copy(targets_far, targets, local.at[5]),
    ]
    first_load = [
        pltpu.make_async_copy(ids_far, ids, local.at[3]),
        pltpu.make_async_copy(tokens_far, tokens, local.at[4]),
    ]
    for copy in first_load:
        copy.start()
    for copy in load:
        copy.start()

    shard_rows = inputs.shape[0] // 8
    mean_ring = Exchange(
        depth, low, mean_at, inputs.shape[1] // 8, part2, hop2, mid2, fin2,
        give2, got2, total.at[core], send2, recv2,
    )
    rings = [
        Exchange(
            row, side, tensor_at, shard_rows, part, hop.at[step], mid, fin.at[step],
            give, got.at[step], error.at[step], send.at[step], recv.at[step],
        )
        for step in range(INNER)
    ]
    near_ring = Exchange(
        row, side, tensor_at, shard_rows, part, None, mid, None,
        give, None, near_error, send3, recv3,
    )
    barrier = pltpu.get_barrier_semaphore()
    peers = rings[0].peers() + mean_ring.peers() + [twin, relay_end, relay_start, turner, turned]
    peers += [((rep + shift) % 16, ten) for shift in (1, 2, 14, 15)]
    for peer in peers:
        pl.semaphore_signal(barrier, inc=1, device_id=peer, device_id_type=MESH)

    rows, width = inputs.shape
    units = hidden.shape[1]
    blocks = 4
    tall = width // blocks
    chunk_rows = rows // 4

    def remote(src, dst, send_sem, recv_sem, device):
        return pltpu.make_async_remote_copy(
            src_ref=src, dst_ref=dst, send_sem=send_sem, recv_sem=recv_sem,
            device_id=device, device_id_type=MESH,
        )

    def chunk_at(chunk):
        return pl.ds(pl.multiple_of(chunk * chunk_rows, chunk_rows), chunk_rows)

    def block_at(j):
        return pl.ds(pl.multiple_of(j * tall, tall), tall)

    def picked(step, chunk, table):
        chosen = ids[step, :, chunk_at(chunk)]
        places = lax.broadcasted_iota(jnp.int32, (rows, chunk_rows), 0)
        mask = jnp.where(chosen == places, 1.0, 0.0).astype(BF16)
        return contract(mask, table[...], 0, 0)

    def fetch(step):
        def some(i, carry):
            inputs[chunk_at(i), :] = picked(step, i, tokens).astype(BF16)
            return carry

        lax.fori_loop(0, 4, some, 0)

    def start_cast(i, carry):
        at = pl.ds(pl.multiple_of(i * 128, 128), 128)
        for m in (0, 1):
            cast[m, at, :] = weights[m, at, :].astype(BF16)
        return carry

    def near_x(i):
        at = chunk_at(i)
        return remote(inputs.at[at], near_inputs.at[at], near_send.at[8 + i], near_recv.at[8 + i], after)

    def near_m(m, j):
        at = block_at(j)
        index = m * blocks + j
        return remote(
            out_box.at[0, m, at], in_box.at[0, m, at], near_send.at[index], near_recv.at[index], after
        )

    def near_shard():
        own = pl.ds(pl.multiple_of(ten * shard_rows, shard_rows), shard_rows)
        return remote(error.at[0, own], near_error.at[own], near_send.at[12], near_recv.at[12], after)

    pieces = [("x", 0, i) for i in range(4)] + [("m", m, j) for m in (1, 0) for j in range(4)]

    def drip():
        if not pieces:
            return
        kind, m, j = pieces.pop(0)
        if (kind, m, j) == ("m", 1, 0):
            load[2].wait()

        @pl.when(ships)
        def _():
            if kind == "x":
                near_x(j).start()
                return

            def decay(i, carry):
                at = pl.ds(pl.multiple_of(j * tall + i * 64, 64), 64)
                out_box[0, m, at, :] = (inner_beta * moment[m, at, :]).astype(BF16)
                return carry

            lax.fori_loop(0, tall // 64, decay, 0)
            near_m(m, j).start()

    def straight(m, j):
        at = block_at(j)
        index = m * blocks + j
        return remote(
            out_box.at[0, m, at], in_box.at[0, m, at], turn_send.at[index], turn_recv.at[index], after
        )

    def turn_first(m, j):
        index, place = m * blocks + j, m * 2 + j // 2
        return remote(
            out_box.at[0, m, block_at(j)], carried.at[place],
            turn_send.at[index], turn_recv.at[8 + place], turner,
        )

    def turn_second(m, j):
        index, place = m * blocks + j, m * 2 + j // 2
        return remote(
            carried.at[place], in_box.at[0, m, block_at(j)],
            turn_send.at[8 + place], turn_recv.at[index], beside,
        )

    def box(m, j):
        at = block_at(j)
        index = m * blocks + j
        return remote(
            out_box.at[1, m, at], in_box.at[1, m, at], box_send.at[index], box_recv.at[index], second
        )

    def leg(hop_index, j):
        src = out_box.at[1, 1, block_at(j)] if hop_index == 0 else relay.at[hop_index - 1, j]
        dst = in_box.at[1, 1, block_at(j)] if hop_index == 2 else relay.at[hop_index, j]
        return remote(
            src, dst, relay_send.at[hop_index, j], relay_recv.at[hop_index, j],
            relay_end if hop_index == 2 else down2,
        )

    def twin_box(j):
        at = block_at(j)
        return remote(twin_out.at[at], twin_in.at[at], twin_send.at[j], twin_recv.at[j], twin)

    for copy in first_load:
        copy.wait()
    fetch(0)
    load[0].wait()
    load[1].wait()
    lax.fori_loop(0, width // 128, start_cast, 0)
    pl.semaphore_wait(barrier, len(peers))
    drip()

    def one_step(step):
        ring = rings[step]

        def forward(source, at, kept, rise):
            pre = jnp.dot(source[at, :], cast[0], preferred_element_type=F32)
            value, tilt = gelu_pair(pre)
            value = value.astype(BF16)
            kept[at, :] = value
            rise[at, :] = tilt
            return value

        def make(chunk):
            value = forward(inputs, chunk_at(chunk), hidden, slope)
            out = contract(value, cast[1], 1, 1)
            part[chunk] = out.astype(BF16).reshape(2, shard_rows, width)

        def idle():
            if step == 0:
                load[3].wait()
            want[...] = picked(step, row, targets).reshape(2, shard_rows, width)

        summed = ring.reduce(make, idle, drip if step == 0 else lambda: None)
        own = pl.ds(pl.multiple_of(ten * shard_rows, shard_rows), shard_rows)
        error[step, own, :] = ((summed - want[side]) * (1.0 / rows)).astype(BF16)

        def pull(source, at, rise, result):
            slide = jnp.dot(source[at, :], cast[1], preferred_element_type=F32)
            result[at, :] = (slide * rise[at, :]).astype(BF16)

        def arrived(chunk):
            pull(error.at[step], chunk_at(chunk), slope, back)

        def near_forward(part_of):
            for i in (part_of * 2, part_of * 2 + 1):
                near_x(i).wait_recv()

            def one(i, carry):
                forward(near_inputs, chunk_at(i), near_hidden, near_slope)
                return carry

            lax.fori_loop(part_of * 2, part_of * 2 + 2, one, 0)

        ring.open()
        if step == 0:

            @pl.when(ships)
            def _():
                near_shard().start()

            drip()

            @pl.when(hears)
            def _():
                near_forward(0)

            drip()
            ring.pass_on()

            @pl.when(hears)
            def _():
                near_shard().wait_recv()
                near_ring.open()

            drip()
            ring.collect(arrived, drip)
            while pieces:
                drip()

            @pl.when(hears)
            def _():
                near_ring.pass_on()
                near_forward(1)

        else:
            ring.pass_on()
            ring.collect(arrived)

        def pass_turn(m, j):
            turn_first(m, j).wait_recv()
            turn_second(m, j).start()

        def update(m, left, right, first, last, ship):
            def one(j, carry):
                at = block_at(j)
                fresh = inner_beta * moment[m, at, :] + contract(left[:, at], right[...], 0, 0)
                moment[m, at, :] = fresh
                moved = fresh if step == 0 else gone[m, at, :] + fresh
                gone[m, at, :] = moved
                if step < 2:
                    kept = weights[m, at, :] - learn_rate * fresh
                    weights[m, at, :] = kept
                if step == 0:

                    @pl.when(jnp.logical_not(ships))
                    def _():
                        out_box[0, m, at, :] = kept.astype(BF16)

                        @pl.when(j % 2 == 0)
                        def _():
                            straight(m, j).start()

                        @pl.when(j % 2 == 1)
                        def _():
                            turn_first(m, j).start()

                if step == 1:
                    out_box[1, m, at, :] = kept.astype(BF16)
                    ship(j).start()
                if step == 2:

                    @pl.when(core == 1 - m)
                    def _():
                        twin_out[at, :] = moved.astype(BF16)
                        twin_box(j).start()

                return carry

            lax.fori_loop(first, last, one, 0)

        def blend(m, at, other):
            mixed = 0.5 * (weights[m, at, :] + other)
            weights[m, at, :] = mixed
            cast[m, at, :] = mixed.astype(BF16)

        if step == 1:
            update(1, error.at[step], hidden, 0, 2, lambda j: leg(0, j))
            update(1, error.at[step], hidden, 2, 4, lambda j: box(1, j))
            update(0, inputs, back, 0, 4, lambda j: box(0, j))
        elif step == 0:
            update(1, error.at[step], hidden, 0, 4, None)

            @pl.when(jnp.logical_not(hears))
            def _():
                pass_turn(1, 1)
                pass_turn(1, 3)

            update(0, inputs, back, 0, 4, None)

            @pl.when(jnp.logical_not(hears))
            def _():
                pass_turn(0, 1)
        else:
            @pl.when(core == 0)
            def _():
                update(1, error.at[step], hidden, 0, 4, None)
                update(0, inputs, back, 0, 4, None)

            @pl.when(core == 1)
            def _():
                update(0, inputs, back, 0, 4, None)
                update(1, error.at[step], hidden, 0, 4, None)

        ring.finish()

        if step == 0:

            @pl.when(ships)
            def _():
                for i in range(4):
                    near_x(i).wait_send()

            fetch(1)

            @pl.when(hears)
            def _():
                near_ring.collect(
                    lambda chunk: pull(near_error, chunk_at(chunk), near_slope, near_back)
                )
                for m in (1, 0):
                    for j in range(blocks):
                        near_m(m, j).wait_recv()
                for m, left, right in ((1, near_error, near_hidden), (0, near_inputs, near_back)):

                    def one(j, carry):
                        at = block_at(j)
                        grad = contract(left[:, at], right[...], 0, 0)
                        began = weights[m, at, :] + learn_rate * moment[m, at, :]
                        near = began - learn_rate * (in_box[0, m, at, :].astype(F32) + grad)
                        blend(m, at, near.astype(BF16).astype(F32))
                        return carry

                    lax.fori_loop(0, blocks, one, 0)
                near_ring.finish_gather()

            @pl.when(jnp.logical_not(hears))
            def _():
                def take_turn(m, j):
                    straight(m, j).wait_recv()
                    blend(m, block_at(j), in_box[0, m, block_at(j), :].astype(F32))

                take_turn(1, 0)
                pass_turn(0, 3)
                take_turn(1, 1)
                take_turn(1, 2)
                take_turn(1, 3)
                take_turn(0, 0)
                take_turn(0, 1)
                take_turn(0, 2)
                take_turn(0, 3)
            @pl.when(ships)
            def _():
                for m in (1, 0):
                    for j in range(blocks):
                        near_m(m, j).wait_send()
                near_shard().wait_send()

        if step == 1:

            def take(m, j, copy):
                copy.wait_recv()
                blend(m, block_at(j), in_box[1, m, block_at(j), :].astype(F32))

            def relay_on(hop_index, j):
                leg(hop_index, j).wait_recv()
                leg(hop_index + 1, j).start()

            fetch(2)
            relay_on(0, 0)
            relay_on(0, 1)
            take(1, 2, box(1, 2))
            relay_on(1, 0)
            take(1, 3, box(1, 3))
            relay_on(1, 1)
            take(0, 0, box(0, 0))
            take(0, 1, box(0, 1))
            take(1, 0, leg(2, 0))
            take(0, 2, box(0, 2))
            take(1, 1, leg(2, 1))
            take(0, 3, box(0, 3))
            for m, j in ((1, 2), (1, 3), (0, 0), (0, 1), (0, 2), (0, 3)):
                box(m, j).wait_send()
            for hop_index in range(3):
                for j in (0, 1):
                    leg(hop_index, j).wait_send()

            @pl.when(jnp.logical_not(ships))
            def _():
                for m in (1, 0):
                    for j in range(blocks):
                        straight(m, j).wait_send()

            @pl.when(jnp.logical_not(hears))
            def _():
                for m in (1, 0):
                    for j in (1, 3):
                        turn_second(m, j).wait_send()

    for step in range(INNER):
        one_step(step)

    store = pltpu.make_async_copy(moment, moment_out.at[0], local.at[2])
    store.start()

    ring = mean_ring

    def join(chunk):
        at = pl.ds(pl.multiple_of(chunk * tall, tall), tall)
        twin_box(chunk).wait_recv()
        both = gone[core, at, :] + twin_in[at, :].astype(F32)
        part2[chunk] = both.astype(BF16).reshape(2, tall // 2, units)

    summed = ring.reduce(join)
    own = pl.ds(pl.multiple_of((depth * 2 + low) * (width // 8), width // 8), width // 8)
    total[core, own, :] = summed.astype(BF16)

    def across(which, chunk):
        at = pl.ds(pl.multiple_of(chunk * tall, tall), tall)
        return pltpu.make_async_remote_copy(
            src_ref=total.at[which, at],
            dst_ref=total.at[which, at],
            send_sem=core_send.at[chunk],
            recv_sem=core_recv.at[chunk],
            device_id=twin,
            device_id_type=MESH,
        )

    ring.open()
    ring.pass_on()
    ring.collect(lambda chunk: across(core, chunk).start())
    for chunk in range(4):
        across(1 - core, chunk).wait_recv()
    save = pltpu.make_async_copy(total, total_out, local.at[0])
    save.start()
    for chunk in range(4):
        across(core, chunk).wait_send()
        twin_box(chunk).wait_send()
    ring.finish()
    save.wait()
    store.wait()


def body(tokens, targets, row_ids, anchor, momentum, slow):
    rows, width = tokens.shape
    units = anchor.shape[2]
    shard, wide = rows // 8, width // 8
    any_spec = pl.BlockSpec(memory_space=pl.ANY)
    hbm_spec = pl.BlockSpec(memory_space=pltpu.HBM)
    dma = pltpu.SemaphoreType.DMA
    ids = row_ids.reshape(INNER, 1, rows)
    ids, tokens, targets = (pltpu.with_memory_space_constraint(x, pltpu.HBM) for x in (ids, tokens, targets))
    moment, total = pl.pallas_call(
        kernel,
        name="outer_round",
        out_shape=(
            jax.ShapeDtypeStruct(momentum.shape, F32),
            jax.ShapeDtypeStruct(anchor.shape, BF16),
        ),
        in_specs=[hbm_spec] * 5,
        out_specs=(any_spec, any_spec),
        scratch_shapes=[
            pltpu.VMEM((INNER, 1, rows), jnp.int32),
            pltpu.VMEM((rows, width), BF16),
            pltpu.VMEM((rows, width), BF16),
            pltpu.VMEM((2, width, units), F32),
            pltpu.VMEM((2, width, units), F32),
            pltpu.VMEM((2, width, units), F32),
            pltpu.VMEM((2, width, units), BF16),
            pltpu.VMEM((2, 2, width, units), BF16),
            pltpu.VMEM((2, 2, width, units), BF16),
            pltpu.VMEM((width, units), BF16),
            pltpu.VMEM((width, units), BF16),
            pltpu.VMEM((rows, width), BF16),
            pltpu.VMEM((rows, units), BF16),
            pltpu.VMEM((rows, units), F32),
            pltpu.VMEM((rows, units), BF16),
            pltpu.VMEM((2, shard, width), F32),
            pltpu.VMEM((rows, width), BF16),
            pltpu.VMEM((rows, units), BF16),
            pltpu.VMEM((rows, units), F32),
            pltpu.VMEM((rows, units), BF16),
            pltpu.VMEM((rows, width), BF16),
            pltpu.VMEM((2, 2, width // 4, units), BF16),
            pltpu.VMEM((4, width // 4, units), BF16),
            pltpu.VMEM((4, 2, shard, width), BF16),
            pltpu.VMEM((INNER, 2, shard, width), BF16),
            pltpu.VMEM((2, shard, width), BF16),
            pltpu.VMEM((INNER, 2, 2, shard, width), BF16),
            pltpu.VMEM((shard, width), BF16),
            pltpu.VMEM((INNER, shard, width), BF16),
            pltpu.VMEM((INNER, rows, width), BF16),
            pltpu.VMEM((4, 2, wide, units), BF16),
            pltpu.VMEM((2, wide, units), BF16),
            pltpu.VMEM((2, wide, units), BF16),
            pltpu.VMEM((2, 2, wide, units), BF16),
            pltpu.VMEM((wide, units), BF16),
            pltpu.VMEM((wide, units), BF16),
            pltpu.VMEM((2, width, units), BF16),
            dma((INNER, 14)),
            dma((INNER, 14)),
            dma((14,)),
            dma((14,)),
            dma((14,)),
            dma((14,)),
            dma((8,)),
            dma((8,)),
            dma((13,)),
            dma((13,)),
            dma((12,)),
            dma((12,)),
            dma((3, 2)),
            dma((3, 2)),
            dma((4,)),
            dma((4,)),
            dma((4,)),
            dma((4,)),
            dma((6,)),
        ],
        compiler_params=pltpu.CompilerParams(
            collective_id=0, has_side_effects=True, vmem_limit_bytes=48 * 1024 * 1024
        ),
    )(ids, tokens, targets, anchor, momentum)
    mean = total.astype(F32) * (1.0 / lax.axis_size("replica"))
    slow_new = slow_beta * slow + mean
    anchor_new = anchor - learn_rate * slow_new
    return (anchor_new, slow_new, moment)


def solution(mesh):
    return jax.shard_map(
        body,
        mesh=mesh,
        in_specs=(
            P("replica", None),
            P("replica", None),
            P("replica", None, None),
            P(None, None, "tensor"),
            P("replica", None, None, "tensor"),
            P(None, None, "tensor"),
        ),
        out_specs=(
            P(None, None, "tensor"),
            P(None, None, "tensor"),
            P("replica", None, None, "tensor"),
        ),
        check_vma=False,
    )
```

```python
import functools

import jax
import jax.numpy as jnp
from jax import lax
from jax.experimental import pallas as pl
from jax.experimental.pallas import tpu as pltpu
from jax.sharding import PartitionSpec as P

INNER = 3
learn_rate = 0.02
inner_beta = 0.9
slow_beta = 0.5

F32 = jnp.float32
BF16 = jnp.bfloat16
MESH = pl.DeviceIdType.MESH


def gelu_pair(pre):
    coeff = 0.7978845608028654
    square = pre * pre
    tanh_val = jnp.tanh(coeff * (pre + 0.044715 * pre * square))
    upper = 0.5 * (1.0 + tanh_val)
    value = pre * upper
    slope = upper + 0.5 * pre * (1.0 - tanh_val * tanh_val) * coeff * (
        1.0 + 3.0 * 0.044715 * square
    )
    return (value, slope)


def contract(a, b, dim_a, dim_b):
    return lax.dot_general(a, b, (((dim_a,), (dim_b,)), ((), ())), preferred_element_type=F32)


class Exchange:
    def __init__(self, pos, half, at, block, part, hop, mid, fin, give, got, full, send, recv):
        self.pos, self.half, self.block = pos, half, block
        self.part, self.hop, self.mid, self.fin = part, hop, mid, fin
        self.give, self.got, self.full, self.send, self.recv = give, got, full, send, recv
        self.far, self.above, self.below = (pos + 2) % 4, (pos + 1) % 4, (pos + 3) % 4
        self.first_of = at(self.above, 0)
        self.second_of = at(self.below, 1)
        self.up, self.down = at(self.above, half), at(self.below, half)
        self.up_across, self.down_across = at(self.above, 1 - half), at(self.below, 1 - half)
        self.pair = at(pos, 1 - half)
        self.sent = []

    def peers(self):
        return [self.up, self.down, self.up_across, self.down_across, self.pair]

    def copy(self, src, dst, index, device, landing=None):
        return pltpu.make_async_remote_copy(
            src_ref=src,
            dst_ref=dst,
            send_sem=self.send.at[index],
            recv_sem=self.recv.at[index if landing is None else landing],
            device_id=device,
            device_id_type=MESH,
        )

    def start(self, src, dst, index, device, landing=None):
        copy = self.copy(src, dst, index, device, landing)
        copy.start()
        self.sent.append(copy)
        return copy

    def reduce(self, make, idle=None, between=lambda: None):
        pos, half, part, fin, mid = self.pos, self.half, self.part, self.fin, self.mid
        make(self.far)
        first_up = self.start(part.at[self.far, 0], self.hop.at[0], 0, self.up)
        first_down = self.start(part.at[self.far, 1], self.hop.at[1], 1, self.down)
        between()
        make(self.above)
        direct_up = self.start(part.at[self.above, 1], fin.at[1, 0], 2, self.up)
        between()
        make(self.below)
        direct_down = self.start(part.at[self.below, 0], fin.at[0, 0], 3, self.down)
        between()
        make(pos)
        between()
        first_up.wait_recv()
        mid[0] = (part[self.above, 0].astype(F32) + self.hop[0].astype(F32)).astype(BF16)
        self.start(mid.at[0], fin.at[half, 1], 4, self.first_of, 4 + half)
        first_down.wait_recv()
        mid[1] = (part[self.below, 1].astype(F32) + self.hop[1].astype(F32)).astype(BF16)
        self.start(mid.at[1], fin.at[half, 1], 5, self.second_of, 4 + half)
        if idle is not None:
            idle()
        direct_up.wait_recv()
        direct_down.wait_recv()
        self.give[...] = self.near_total(1 - half).astype(BF16)
        last = self.start(self.give, self.got, 6, self.pair)
        mine = self.near_total(half)
        for plane in (0, 1):
            self.copy(mid.at[0], fin.at[plane, 1], 4, self.first_of, 4 + plane).wait_recv()
        mine = mine + fin[0, 1].astype(F32) + fin[1, 1].astype(F32)
        last.wait_recv()
        return mine + self.got[...].astype(F32)

    def near_total(self, half):
        return self.part[self.pos, half].astype(F32) + self.fin[half, 0].astype(F32)

    def slot(self, chunk, half):
        return self.full.at[pl.ds(pl.multiple_of((chunk * 2 + half) * self.block, self.block), self.block)]

    def open(self):
        own = self.slot(self.pos, self.half)
        self.start(own, own, 8, self.up)
        self.start(own, own, 9, self.down)
        self.start(own, own, 11, self.down_across)
        self.start(own, own, 10, self.up_across)
        self.start(own, own, 7, self.pair)

    def await_slot(self, chunk, half, index):
        slot = self.slot(chunk, half)
        self.copy(slot, slot, index, self.pair).wait_recv()
        return slot

    def pass_on(self):
        early = self.await_slot(self.below, self.half, 8)
        self.start(early, early, 12, self.up)
        late = self.await_slot(self.above, 1 - self.half, 11)
        self.start(late, late, 13, self.down)

    def collect(self, arrived, between=lambda: None):
        half = self.half
        self.await_slot(self.pos, 1 - half, 7)
        arrived(self.pos)
        between()
        self.await_slot(self.above, half, 9)
        arrived(self.above)
        between()
        self.await_slot(self.below, 1 - half, 10)
        arrived(self.below)
        between()
        self.await_slot(self.far, half, 12)
        self.await_slot(self.far, 1 - half, 13)
        arrived(self.far)

    def finish(self):
        for copy in self.sent:
            copy.wait_send()

    def finish_gather(self):
        for index in range(7, 14):
            slot = self.slot(self.pos, self.half)
            self.copy(slot, slot, index, self.pair).wait_send()


def kernel(
    ids_far, tokens_far, targets_far, anchor, momentum,
    moment_out, total_out,
    ids, tokens, targets, weights, moment, gone, cast, out_box, in_box, twin_out, twin_in,
    inputs, hidden, slope, back, want,
    near_inputs, near_hidden, near_slope, near_back, near_error, relay,
    part, hop, mid, fin, give, got, error,
    part2, hop2, mid2, fin2, give2, got2, total,
    send, recv, send2, recv2, send3, recv3, box_send, box_recv, near_send, near_recv, turn_send, turn_recv,
    relay_send, relay_recv, twin_send, twin_recv, core_send, core_recv, local,
):
    rep, ten = lax.axis_index("replica"), lax.axis_index("tensor")
    row, side = ten // 2, ten % 2
    low, depth, core = rep // 8, (rep // 2) % 4, rep % 2

    def plane(shift):
        return low * 8 + (depth + shift) % 4 * 2 + core

    def tensor_at(pos, half):
        return (rep, pos * 2 + half)

    def mean_at(pos, half):
        return (half * 8 + pos * 2 + core, ten)

    up2, down2 = (plane(1), ten), (plane(3), ten)
    twin = (low * 8 + depth * 2 + 1 - core, ten)
    after, second = ((rep + 1) % 16, ten), ((rep + 2) % 16, ten)
    relay_end = ((plane(2) + 2) % 16, ten)
    past = (rep + 14) % 16
    ships = (depth != 3) | (core != 1)
    hears = (depth != 0) | (core != 0)
    relay_start = (past // 8 * 8 + ((past // 2) % 4 + 2) % 4 * 2 + core, ten)

    load = [
        pltpu.make_async_copy(anchor.at[0], weights.at[0], local.at[0]),
        pltpu.make_async_copy(anchor.at[1], weights.at[1], local.at[1]),
        pltpu.make_async_copy(momentum.at[0], moment, local.at[2]),
        pltpu.make_async_copy(targets_far, targets, local.at[5]),
    ]
    first_load = [
        pltpu.make_async_copy(ids_far, ids, local.at[3]),
        pltpu.make_async_copy(tokens_far, tokens, local.at[4]),
    ]
    for copy in first_load:
        copy.start()
    for copy in load:
        copy.start()

    shard_rows = inputs.shape[0] // 8
    mean_ring = Exchange(
        depth, low, mean_at, inputs.shape[1] // 8, part2, hop2, mid2, fin2,
        give2, got2, total.at[core], send2, recv2,
    )
    rings = [
        Exchange(
            row, side, tensor_at, shard_rows, part, hop.at[step], mid, fin.at[step],
            give, got.at[step], error.at[step], send.at[step], recv.at[step],
        )
        for step in range(INNER)
    ]
    near_ring = Exchange(
        row, side, tensor_at, shard_rows, part, None, mid, None,
        give, None, near_error, send3, recv3,
    )
    barrier = pltpu.get_barrier_semaphore()
    peers = rings[0].peers() + mean_ring.peers() + [twin, relay_end, relay_start]
    peers += [((rep + shift) % 16, ten) for shift in (1, 2, 14, 15)]
    for peer in peers:
        pl.semaphore_signal(barrier, inc=1, device_id=peer, device_id_type=MESH)

    rows, width = inputs.shape
    units = hidden.shape[1]
    blocks = 4
    tall = width // blocks
    chunk_rows = rows // 4

    def remote(src, dst, send_sem, recv_sem, device):
        return pltpu.make_async_remote_copy(
            src_ref=src, dst_ref=dst, send_sem=send_sem, recv_sem=recv_sem,
            device_id=device, device_id_type=MESH,
        )

    def chunk_at(chunk):
        return pl.ds(pl.multiple_of(chunk * chunk_rows, chunk_rows), chunk_rows)

    def block_at(j):
        return pl.ds(pl.multiple_of(j * tall, tall), tall)

    def picked(step, chunk, table):
        chosen = ids[step, :, chunk_at(chunk)]
        places = lax.broadcasted_iota(jnp.int32, (rows, chunk_rows), 0)
        mask = jnp.where(chosen == places, 1.0, 0.0).astype(BF16)
        return contract(mask, table[...], 0, 0)

    def fetch(step):
        def some(i, carry):
            inputs[chunk_at(i), :] = picked(step, i, tokens).astype(BF16)
            return carry

        lax.fori_loop(0, 4, some, 0)

    def start_cast(i, carry):
        at = pl.ds(pl.multiple_of(i * 128, 128), 128)
        for m in (0, 1):
            cast[m, at, :] = weights[m, at, :].astype(BF16)
        return carry

    def near_x(i):
        at = chunk_at(i)
        return remote(inputs.at[at], near_inputs.at[at], near_send.at[8 + i], near_recv.at[8 + i], after)

    def near_m(m, j):
        at = block_at(j)
        index = m * blocks + j
        return remote(
            out_box.at[0, m, at], in_box.at[0, m, at], near_send.at[index], near_recv.at[index], after
        )

    def near_shard():
        own = pl.ds(pl.multiple_of(ten * shard_rows, shard_rows), shard_rows)
        return remote(error.at[0, own], near_error.at[own], near_send.at[12], near_recv.at[12], after)

    pieces = [("x", 0, i) for i in range(4)] + [("m", m, j) for m in (1, 0) for j in range(4)]

    def drip():
        if not pieces:
            return
        kind, m, j = pieces.pop(0)
        if (kind, m, j) == ("m", 1, 0):
            load[2].wait()

        @pl.when(ships)
        def _():
            if kind == "x":
                near_x(j).start()
                return

            def decay(i, carry):
                at = pl.ds(pl.multiple_of(j * tall + i * 64, 64), 64)
                out_box[0, m, at, :] = (inner_beta * moment[m, at, :]).astype(BF16)
                return carry

            lax.fori_loop(0, tall // 64, decay, 0)
            near_m(m, j).start()

    def straight(m, j):
        at = block_at(j)
        index = m * blocks + j
        return remote(
            out_box.at[0, m, at], in_box.at[0, m, at], turn_send.at[index], turn_recv.at[index], after
        )

    def box(m, j):
        at = block_at(j)
        index = m * blocks + j
        return remote(
            out_box.at[1, m, at], in_box.at[1, m, at], box_send.at[index], box_recv.at[index], second
        )

    def leg(hop_index, j):
        src = out_box.at[1, 1, block_at(j)] if hop_index == 0 else relay.at[hop_index - 1, j]
        dst = in_box.at[1, 1, block_at(j)] if hop_index == 2 else relay.at[hop_index, j]
        return remote(
            src, dst, relay_send.at[hop_index, j], relay_recv.at[hop_index, j],
            relay_end if hop_index == 2 else down2,
        )

    def twin_box(j):
        at = block_at(j)
        return remote(twin_out.at[at], twin_in.at[at], twin_send.at[j], twin_recv.at[j], twin)

    for copy in first_load:
        copy.wait()
    fetch(0)
    load[0].wait()
    load[1].wait()
    lax.fori_loop(0, width // 128, start_cast, 0)
    pl.semaphore_wait(barrier, len(peers))
    drip()

    def one_step(step):
        ring = rings[step]

        def forward(source, at, kept, rise):
            pre = jnp.dot(source[at, :], cast[0], preferred_element_type=F32)
            value, tilt = gelu_pair(pre)
            value = value.astype(BF16)
            kept[at, :] = value
            rise[at, :] = tilt
            return value

        def make(chunk):
            value = forward(inputs, chunk_at(chunk), hidden, slope)
            out = contract(value, cast[1], 1, 1)
            part[chunk] = out.astype(BF16).reshape(2, shard_rows, width)

        def idle():
            if step == 0:
                load[3].wait()
            want[...] = picked(step, row, targets).reshape(2, shard_rows, width)

        summed = ring.reduce(make, idle, drip if step == 0 else lambda: None)
        own = pl.ds(pl.multiple_of(ten * shard_rows, shard_rows), shard_rows)
        error[step, own, :] = ((summed - want[side]) * (1.0 / rows)).astype(BF16)

        def pull(source, at, rise, result):
            slide = jnp.dot(source[at, :], cast[1], preferred_element_type=F32)
            result[at, :] = (slide * rise[at, :]).astype(BF16)

        def arrived(chunk):
            pull(error.at[step], chunk_at(chunk), slope, back)

        def near_forward(part_of):
            for i in (part_of * 2, part_of * 2 + 1):
                near_x(i).wait_recv()

            def one(i, carry):
                forward(near_inputs, chunk_at(i), near_hidden, near_slope)
                return carry

            lax.fori_loop(part_of * 2, part_of * 2 + 2, one, 0)

        ring.open()
        if step == 0:

            @pl.when(ships)
            def _():
                near_shard().start()

            drip()

            @pl.when(hears)
            def _():
                near_forward(0)

            drip()
            ring.pass_on()

            @pl.when(hears)
            def _():
                near_shard().wait_recv()
                near_ring.open()

            drip()
            ring.collect(arrived, drip)
            while pieces:
                drip()

            @pl.when(hears)
            def _():
                near_ring.pass_on()
                near_forward(1)

        else:
            ring.pass_on()
            ring.collect(arrived)

        def update(m, left, right, first, last, ship):
            def one(j, carry):
                at = block_at(j)
                fresh = inner_beta * moment[m, at, :] + contract(left[:, at], right[...], 0, 0)
                moment[m, at, :] = fresh
                moved = fresh if step == 0 else gone[m, at, :] + fresh
                gone[m, at, :] = moved
                if step < 2:
                    kept = weights[m, at, :] - learn_rate * fresh
                    weights[m, at, :] = kept
                if step == 0:

                    @pl.when(jnp.logical_not(ships))
                    def _():
                        out_box[0, m, at, :] = kept.astype(BF16)
                        straight(m, j).start()

                if step == 1:
                    out_box[1, m, at, :] = kept.astype(BF16)
                    ship(j).start()
                if step == 2:

                    @pl.when(core == 1 - m)
                    def _():
                        twin_out[at, :] = moved.astype(BF16)
                        twin_box(j).start()

                return carry

            lax.fori_loop(first, last, one, 0)

        def blend(m, at, other):
            mixed = 0.5 * (weights[m, at, :] + other)
            weights[m, at, :] = mixed
            cast[m, at, :] = mixed.astype(BF16)

        if step == 1:
            update(1, error.at[step], hidden, 0, 2, lambda j: leg(0, j))
            update(1, error.at[step], hidden, 2, 4, lambda j: box(1, j))
            update(0, inputs, back, 0, 4, lambda j: box(0, j))
        elif step == 0:
            update(1, error.at[step], hidden, 0, 4, None)
            update(0, inputs, back, 0, 4, None)
        else:
            @pl.when(core == 0)
            def _():
                update(1, error.at[step], hidden, 0, 4, None)
                update(0, inputs, back, 0, 4, None)

            @pl.when(core == 1)
            def _():
                update(0, inputs, back, 0, 4, None)
                update(1, error.at[step], hidden, 0, 4, None)

        ring.finish()

        if step == 0:

            @pl.when(ships)
            def _():
                for i in range(4):
                    near_x(i).wait_send()

            fetch(1)

            @pl.when(hears)
            def _():
                near_ring.collect(
                    lambda chunk: pull(near_error, chunk_at(chunk), near_slope, near_back)
                )
                for m in (1, 0):
                    for j in range(blocks):
                        near_m(m, j).wait_recv()
                for m, left, right in ((1, near_error, near_hidden), (0, near_inputs, near_back)):

                    def one(j, carry):
                        at = block_at(j)
                        grad = contract(left[:, at], right[...], 0, 0)
                        began = weights[m, at, :] + learn_rate * moment[m, at, :]
                        near = began - learn_rate * (in_box[0, m, at, :].astype(F32) + grad)
                        blend(m, at, near.astype(BF16).astype(F32))
                        return carry

                    lax.fori_loop(0, blocks, one, 0)
                near_ring.finish_gather()

            @pl.when(jnp.logical_not(hears))
            def _():
                def take_turn(m, j):
                    straight(m, j).wait_recv()
                    blend(m, block_at(j), in_box[0, m, block_at(j), :].astype(F32))

                for m in (1, 0):
                    for j in range(blocks):
                        take_turn(m, j)
            @pl.when(ships)
            def _():
                for m in (1, 0):
                    for j in range(blocks):
                        near_m(m, j).wait_send()
                near_shard().wait_send()

        if step == 1:

            def take(m, j, copy):
                copy.wait_recv()
                blend(m, block_at(j), in_box[1, m, block_at(j), :].astype(F32))

            def relay_on(hop_index, j):
                leg(hop_index, j).wait_recv()
                leg(hop_index + 1, j).start()

            fetch(2)
            relay_on(0, 0)
            relay_on(0, 1)
            take(1, 2, box(1, 2))
            relay_on(1, 0)
            take(1, 3, box(1, 3))
            relay_on(1, 1)
            take(0, 0, box(0, 0))
            take(0, 1, box(0, 1))
            take(1, 0, leg(2, 0))
            take(0, 2, box(0, 2))
            take(1, 1, leg(2, 1))
            take(0, 3, box(0, 3))
            for m, j in ((1, 2), (1, 3), (0, 0), (0, 1), (0, 2), (0, 3)):
                box(m, j).wait_send()
            for hop_index in range(3):
                for j in (0, 1):
                    leg(hop_index, j).wait_send()

            @pl.when(jnp.logical_not(ships))
            def _():
                for m in (1, 0):
                    for j in range(blocks):
                        straight(m, j).wait_send()

    for step in range(INNER):
        one_step(step)

    store = pltpu.make_async_copy(moment, moment_out.at[0], local.at[2])
    store.start()

    ring = mean_ring

    def join(chunk):
        at = pl.ds(pl.multiple_of(chunk * tall, tall), tall)
        twin_box(chunk).wait_recv()
        both = gone[core, at, :] + twin_in[at, :].astype(F32)
        part2[chunk] = both.astype(BF16).reshape(2, tall // 2, units)

    summed = ring.reduce(join)
    own = pl.ds(pl.multiple_of((depth * 2 + low) * (width // 8), width // 8), width // 8)
    total[core, own, :] = summed.astype(BF16)

    def across(which, chunk):
        at = pl.ds(pl.multiple_of(chunk * tall, tall), tall)
        return pltpu.make_async_remote_copy(
            src_ref=total.at[which, at],
            dst_ref=total.at[which, at],
            send_sem=core_send.at[chunk],
            recv_sem=core_recv.at[chunk],
            device_id=twin,
            device_id_type=MESH,
        )

    ring.open()
    ring.pass_on()
    ring.collect(lambda chunk: across(core, chunk).start())
    saves = [
        pltpu.make_async_copy(total.at[which], total_out.at[which], local.at[place])
        for place, which in enumerate((core, 1 - core))
    ]
    saves[0].start()
    for chunk in range(4):
        across(1 - core, chunk).wait_recv()
    saves[1].start()
    for chunk in range(4):
        across(core, chunk).wait_send()
        twin_box(chunk).wait_send()
    ring.finish()
    for save in saves:
        save.wait()
    store.wait()


def body(tokens, targets, row_ids, anchor, momentum, slow):
    rows, width = tokens.shape
    units = anchor.shape[2]
    shard, wide = rows // 8, width // 8
    any_spec = pl.BlockSpec(memory_space=pl.ANY)
    hbm_spec = pl.BlockSpec(memory_space=pltpu.HBM)
    dma = pltpu.SemaphoreType.DMA
    ids = row_ids.reshape(INNER, 1, rows)
    ids, tokens, targets = (pltpu.with_memory_space_constraint(x, pltpu.HBM) for x in (ids, tokens, targets))
    moment, total = pl.pallas_call(
        kernel,
        name="outer_round",
        out_shape=(
            jax.ShapeDtypeStruct(momentum.shape, F32),
            jax.ShapeDtypeStruct(anchor.shape, BF16),
        ),
        in_specs=[hbm_spec] * 5,
        out_specs=(any_spec, any_spec),
        scratch_shapes=[
            pltpu.VMEM((INNER, 1, rows), jnp.int32),
            pltpu.VMEM((rows, width), BF16),
            pltpu.VMEM((rows, width), BF16),
            pltpu.VMEM((2, width, units), F32),
            pltpu.VMEM((2, width, units), F32),
            pltpu.VMEM((2, width, units), F32),
            pltpu.VMEM((2, width, units), BF16),
            pltpu.VMEM((2, 2, width, units), BF16),
            pltpu.VMEM((2, 2, width, units), BF16),
            pltpu.VMEM((width, units), BF16),
            pltpu.VMEM((width, units), BF16),
            pltpu.VMEM((rows, width), BF16),
            pltpu.VMEM((rows, units), BF16),
            pltpu.VMEM((rows, units), F32),
            pltpu.VMEM((rows, units), BF16),
            pltpu.VMEM((2, shard, width), F32),
            pltpu.VMEM((rows, width), BF16),
            pltpu.VMEM((rows, units), BF16),
            pltpu.VMEM((rows, units), F32),
            pltpu.VMEM((rows, units), BF16),
            pltpu.VMEM((rows, width), BF16),
            pltpu.VMEM((2, 2, width // 4, units), BF16),
            pltpu.VMEM((4, 2, shard, width), BF16),
            pltpu.VMEM((INNER, 2, shard, width), BF16),
            pltpu.VMEM((2, shard, width), BF16),
            pltpu.VMEM((INNER, 2, 2, shard, width), BF16),
            pltpu.VMEM((shard, width), BF16),
            pltpu.VMEM((INNER, shard, width), BF16),
            pltpu.VMEM((INNER, rows, width), BF16),
            pltpu.VMEM((4, 2, wide, units), BF16),
            pltpu.VMEM((2, wide, units), BF16),
            pltpu.VMEM((2, wide, units), BF16),
            pltpu.VMEM((2, 2, wide, units), BF16),
            pltpu.VMEM((wide, units), BF16),
            pltpu.VMEM((wide, units), BF16),
            pltpu.VMEM((2, width, units), BF16),
            dma((INNER, 14)),
            dma((INNER, 14)),
            dma((14,)),
            dma((14,)),
            dma((14,)),
            dma((14,)),
            dma((8,)),
            dma((8,)),
            dma((13,)),
            dma((13,)),
            dma((8,)),
            dma((8,)),
            dma((3, 2)),
            dma((3, 2)),
            dma((4,)),
            dma((4,)),
            dma((4,)),
            dma((4,)),
            dma((6,)),
        ],
        compiler_params=pltpu.CompilerParams(
            collective_id=0, has_side_effects=True, vmem_limit_bytes=48 * 1024 * 1024
        ),
    )(ids, tokens, targets, anchor, momentum)
    mean = total.astype(F32) * (1.0 / lax.axis_size("replica"))
    slow_new = slow_beta * slow + mean
    anchor_new = anchor - learn_rate * slow_new
    return (anchor_new, slow_new, moment)


def solution(mesh):
    return jax.shard_map(
        body,
        mesh=mesh,
        in_specs=(
            P("replica", None),
            P("replica", None),
            P("replica", None, None),
            P(None, None, "tensor"),
            P("replica", None, None, "tensor"),
            P(None, None, "tensor"),
        ),
        out_specs=(
            P(None, None, "tensor"),
            P(None, None, "tensor"),
            P("replica", None, None, "tensor"),
        ),
        check_vma=False,
    )
```

```python
import functools

import jax
import jax.numpy as jnp
from jax import lax
from jax.experimental import pallas as pl
from jax.experimental.pallas import tpu as pltpu
from jax.sharding import PartitionSpec as P

INNER = 3
learn_rate = 0.02
inner_beta = 0.9
slow_beta = 0.5

F32 = jnp.float32
BF16 = jnp.bfloat16
MESH = pl.DeviceIdType.MESH


def gelu_pair(pre):
    coeff = 0.7978845608028654
    square = pre * pre
    tanh_val = jnp.tanh(coeff * (pre + 0.044715 * pre * square))
    upper = 0.5 * (1.0 + tanh_val)
    value = pre * upper
    slope = upper + 0.5 * pre * (1.0 - tanh_val * tanh_val) * coeff * (
        1.0 + 3.0 * 0.044715 * square
    )
    return (value, slope)


def contract(a, b, dim_a, dim_b):
    return lax.dot_general(a, b, (((dim_a,), (dim_b,)), ((), ())), preferred_element_type=F32)


class Exchange:
    def __init__(self, pos, half, at, block, part, hop, mid, fin, give, got, full, send, recv):
        self.pos, self.half, self.block = pos, half, block
        self.part, self.hop, self.mid, self.fin = part, hop, mid, fin
        self.give, self.got, self.full, self.send, self.recv = give, got, full, send, recv
        self.far, self.above, self.below = (pos + 2) % 4, (pos + 1) % 4, (pos + 3) % 4
        self.first_of = at(self.above, 0)
        self.second_of = at(self.below, 1)
        self.up, self.down = at(self.above, half), at(self.below, half)
        self.up_across, self.down_across = at(self.above, 1 - half), at(self.below, 1 - half)
        self.pair = at(pos, 1 - half)
        self.sent = []

    def peers(self):
        return [self.up, self.down, self.up_across, self.down_across, self.pair]

    def copy(self, src, dst, index, device, landing=None):
        return pltpu.make_async_remote_copy(
            src_ref=src,
            dst_ref=dst,
            send_sem=self.send.at[index],
            recv_sem=self.recv.at[index if landing is None else landing],
            device_id=device,
            device_id_type=MESH,
        )

    def start(self, src, dst, index, device, landing=None):
        copy = self.copy(src, dst, index, device, landing)
        copy.start()
        self.sent.append(copy)
        return copy

    def reduce(self, make, idle=None, between=lambda: None):
        pos, half, part, fin, mid = self.pos, self.half, self.part, self.fin, self.mid
        make(self.far)
        first_up = self.start(part.at[self.far, 0], self.hop.at[0], 0, self.up)
        first_down = self.start(part.at[self.far, 1], self.hop.at[1], 1, self.down)
        between()
        make(self.above)
        direct_up = self.start(part.at[self.above, 1], fin.at[1, 0], 2, self.up)
        between()
        make(self.below)
        direct_down = self.start(part.at[self.below, 0], fin.at[0, 0], 3, self.down)
        between()
        make(pos)
        between()
        first_up.wait_recv()
        mid[0] = (part[self.above, 0].astype(F32) + self.hop[0].astype(F32)).astype(BF16)
        self.start(mid.at[0], fin.at[half, 1], 4, self.first_of, 4 + half)
        first_down.wait_recv()
        mid[1] = (part[self.below, 1].astype(F32) + self.hop[1].astype(F32)).astype(BF16)
        self.start(mid.at[1], fin.at[half, 1], 5, self.second_of, 4 + half)
        if idle is not None:
            idle()
        direct_up.wait_recv()
        direct_down.wait_recv()
        self.give[...] = self.near_total(1 - half).astype(BF16)
        last = self.start(self.give, self.got, 6, self.pair)
        mine = self.near_total(half)
        for plane in (0, 1):
            self.copy(mid.at[0], fin.at[plane, 1], 4, self.first_of, 4 + plane).wait_recv()
        mine = mine + fin[0, 1].astype(F32) + fin[1, 1].astype(F32)
        last.wait_recv()
        return mine + self.got[...].astype(F32)

    def near_total(self, half):
        return self.part[self.pos, half].astype(F32) + self.fin[half, 0].astype(F32)

    def slot(self, chunk, half):
        return self.full.at[pl.ds(pl.multiple_of((chunk * 2 + half) * self.block, self.block), self.block)]

    def open(self):
        own = self.slot(self.pos, self.half)
        self.start(own, own, 8, self.up)
        self.start(own, own, 9, self.down)
        self.start(own, own, 11, self.down_across)
        self.start(own, own, 10, self.up_across)
        self.start(own, own, 7, self.pair)

    def await_slot(self, chunk, half, index):
        slot = self.slot(chunk, half)
        self.copy(slot, slot, index, self.pair).wait_recv()
        return slot

    def pass_on(self):
        early = self.await_slot(self.below, self.half, 8)
        self.start(early, early, 12, self.up)
        late = self.await_slot(self.above, 1 - self.half, 11)
        self.start(late, late, 13, self.down)

    def collect(self, arrived, between=lambda: None):
        half = self.half
        self.await_slot(self.pos, 1 - half, 7)
        arrived(self.pos)
        between()
        self.await_slot(self.above, half, 9)
        arrived(self.above)
        between()
        self.await_slot(self.below, 1 - half, 10)
        arrived(self.below)
        between()
        self.await_slot(self.far, half, 12)
        self.await_slot(self.far, 1 - half, 13)
        arrived(self.far)

    def finish(self):
        for copy in self.sent:
            copy.wait_send()

    def finish_gather(self):
        for index in range(7, 14):
            slot = self.slot(self.pos, self.half)
            self.copy(slot, slot, index, self.pair).wait_send()


def kernel(
    ids_far, tokens_far, targets_far, anchor, momentum,
    moment_out, total_out,
    ids, tokens, targets, weights, moment, gone, cast, out_box, in_box, twin_out, twin_in,
    inputs, hidden, slope, back, want,
    near_inputs, near_hidden, near_slope, near_back, near_error, relay, carried,
    part, hop, mid, fin, give, got, error,
    part2, hop2, mid2, fin2, give2, got2, total,
    send, recv, send2, recv2, send3, recv3, box_send, box_recv, near_send, near_recv, turn_send, turn_recv,
    relay_send, relay_recv, twin_send, twin_recv, core_send, core_recv, local,
):
    rep, ten = lax.axis_index("replica"), lax.axis_index("tensor")
    row, side = ten // 2, ten % 2
    low, depth, core = rep // 8, (rep // 2) % 4, rep % 2

    def plane(shift):
        return low * 8 + (depth + shift) % 4 * 2 + core

    def tensor_at(pos, half):
        return (rep, pos * 2 + half)

    def mean_at(pos, half):
        return (half * 8 + pos * 2 + core, ten)

    up2, down2 = (plane(1), ten), (plane(3), ten)
    twin = (low * 8 + depth * 2 + 1 - core, ten)
    after, second = ((rep + 1) % 16, ten), ((rep + 2) % 16, ten)
    relay_end = ((plane(2) + 2) % 16, ten)
    past = (rep + 14) % 16
    ships = (depth != 3) | (core != 1)
    hears = (depth != 0) | (core != 0)
    turner = (low * 8 + (depth + 1) % 4 * 2 + 1 - core, ten)
    turned = (low * 8 + (depth + 3) % 4 * 2 + 1 - core, ten)
    beside = ((1 - low) * 8 + depth * 2 + core, ten)
    relay_start = (past // 8 * 8 + ((past // 2) % 4 + 2) % 4 * 2 + core, ten)

    load = [
        pltpu.make_async_copy(anchor.at[0], weights.at[0], local.at[0]),
        pltpu.make_async_copy(anchor.at[1], weights.at[1], local.at[1]),
        pltpu.make_async_copy(momentum.at[0], moment, local.at[2]),
        pltpu.make_async_copy(targets_far, targets, local.at[5]),
    ]
    first_load = [
        pltpu.make_async_copy(ids_far, ids, local.at[3]),
        pltpu.make_async_copy(tokens_far, tokens, local.at[4]),
    ]
    for copy in first_load:
        copy.start()
    for copy in load:
        copy.start()

    shard_rows = inputs.shape[0] // 8
    mean_ring = Exchange(
        depth, low, mean_at, inputs.shape[1] // 8, part2, hop2, mid2, fin2,
        give2, got2, total.at[core], send2, recv2,
    )
    rings = [
        Exchange(
            row, side, tensor_at, shard_rows, part, hop.at[step], mid, fin.at[step],
            give, got.at[step], error.at[step], send.at[step], recv.at[step],
        )
        for step in range(INNER)
    ]
    near_ring = Exchange(
        row, side, tensor_at, shard_rows, part, None, mid, None,
        give, None, near_error, send3, recv3,
    )
    barrier = pltpu.get_barrier_semaphore()
    peers = rings[0].peers() + mean_ring.peers() + [twin, relay_end, relay_start, turner, turned]
    peers += [((rep + shift) % 16, ten) for shift in (1, 2, 14, 15)]
    for peer in peers:
        pl.semaphore_signal(barrier, inc=1, device_id=peer, device_id_type=MESH)

    rows, width = inputs.shape
    units = hidden.shape[1]
    blocks = 4
    tall = width // blocks
    chunk_rows = rows // 4

    def remote(src, dst, send_sem, recv_sem, device):
        return pltpu.make_async_remote_copy(
            src_ref=src, dst_ref=dst, send_sem=send_sem, recv_sem=recv_sem,
            device_id=device, device_id_type=MESH,
        )

    def chunk_at(chunk):
        return pl.ds(pl.multiple_of(chunk * chunk_rows, chunk_rows), chunk_rows)

    def block_at(j):
        return pl.ds(pl.multiple_of(j * tall, tall), tall)

    def picked(step, chunk, table):
        chosen = ids[step, :, chunk_at(chunk)]
        places = lax.broadcasted_iota(jnp.int32, (rows, chunk_rows), 0)
        mask = jnp.where(chosen == places, 1.0, 0.0).astype(BF16)
        return contract(mask, table[...], 0, 0)

    def fetch(step):
        def some(i, carry):
            inputs[chunk_at(i), :] = picked(step, i, tokens).astype(BF16)
            return carry

        lax.fori_loop(0, 4, some, 0)

    def start_cast(i, carry):
        at = pl.ds(pl.multiple_of(i * 128, 128), 128)
        for m in (0, 1):
            cast[m, at, :] = weights[m, at, :].astype(BF16)
        return carry

    def near_x(i):
        at = chunk_at(i)
        return remote(inputs.at[at], near_inputs.at[at], near_send.at[8 + i], near_recv.at[8 + i], after)

    def near_m(m, j):
        at = block_at(j)
        index = m * blocks + j
        return remote(
            out_box.at[0, m, at], in_box.at[0, m, at], near_send.at[index], near_recv.at[index], after
        )

    def near_shard():
        own = pl.ds(pl.multiple_of(ten * shard_rows, shard_rows), shard_rows)
        return remote(error.at[0, own], near_error.at[own], near_send.at[12], near_recv.at[12], after)

    pieces = [("x", 0, i) for i in range(4)] + [("m", m, j) for m in (1, 0) for j in range(4)]

    def drip():
        if not pieces:
            return
        kind, m, j = pieces.pop(0)
        if (kind, m, j) == ("m", 1, 0):
            load[2].wait()

        @pl.when(ships)
        def _():
            if kind == "x":
                near_x(j).start()
                return

            def decay(i, carry):
                at = pl.ds(pl.multiple_of(j * tall + i * 64, 64), 64)
                out_box[0, m, at, :] = (inner_beta * moment[m, at, :]).astype(BF16)
                return carry

            lax.fori_loop(0, tall // 64, decay, 0)
            near_m(m, j).start()

    def turn_first(m, j):
        place = m * blocks + j
        return remote(
            out_box.at[0, m, block_at(j)], carried.at[place],
            turn_send.at[place], turn_recv.at[8 + place], turner,
        )

    def turn_second(m, j):
        place = m * blocks + j
        return remote(
            carried.at[place], in_box.at[0, m, block_at(j)],
            turn_send.at[8 + place], turn_recv.at[place], beside,
        )

    def box(m, j):
        at = block_at(j)
        index = m * blocks + j
        return remote(
            out_box.at[1, m, at], in_box.at[1, m, at], box_send.at[index], box_recv.at[index], second
        )

    def leg(hop_index, j):
        src = out_box.at[1, 1, block_at(j)] if hop_index == 0 else relay.at[hop_index - 1, j]
        dst = in_box.at[1, 1, block_at(j)] if hop_index == 2 else relay.at[hop_index, j]
        return remote(
            src, dst, relay_send.at[hop_index, j], relay_recv.at[hop_index, j],
            relay_end if hop_index == 2 else down2,
        )

    def twin_box(j):
        at = block_at(j)
        return remote(twin_out.at[at], twin_in.at[at], twin_send.at[j], twin_recv.at[j], twin)

    for copy in first_load:
        copy.wait()
    fetch(0)
    load[0].wait()
    load[1].wait()
    lax.fori_loop(0, width // 128, start_cast, 0)
    pl.semaphore_wait(barrier, len(peers))
    drip()

    def one_step(step):
        ring = rings[step]

        def forward(source, at, kept, rise):
            pre = jnp.dot(source[at, :], cast[0], preferred_element_type=F32)
            value, tilt = gelu_pair(pre)
            value = value.astype(BF16)
            kept[at, :] = value
            rise[at, :] = tilt
            return value

        def make(chunk):
            value = forward(inputs, chunk_at(chunk), hidden, slope)
            out = contract(value, cast[1], 1, 1)
            part[chunk] = out.astype(BF16).reshape(2, shard_rows, width)

        def idle():
            if step == 0:
                load[3].wait()
            want[...] = picked(step, row, targets).reshape(2, shard_rows, width)

        summed = ring.reduce(make, idle, drip if step == 0 else lambda: None)
        own = pl.ds(pl.multiple_of(ten * shard_rows, shard_rows), shard_rows)
        error[step, own, :] = ((summed - want[side]) * (1.0 / rows)).astype(BF16)

        def pull(source, at, rise, result):
            slide = jnp.dot(source[at, :], cast[1], preferred_element_type=F32)
            result[at, :] = (slide * rise[at, :]).astype(BF16)

        def arrived(chunk):
            pull(error.at[step], chunk_at(chunk), slope, back)

        def near_forward(part_of):
            for i in (part_of * 2, part_of * 2 + 1):
                near_x(i).wait_recv()

            def one(i, carry):
                forward(near_inputs, chunk_at(i), near_hidden, near_slope)
                return carry

            lax.fori_loop(part_of * 2, part_of * 2 + 2, one, 0)

        ring.open()
        if step == 0:

            @pl.when(ships)
            def _():
                near_shard().start()

            drip()

            @pl.when(hears)
            def _():
                near_forward(0)

            drip()
            ring.pass_on()

            @pl.when(hears)
            def _():
                near_shard().wait_recv()
                near_ring.open()

            drip()
            ring.collect(arrived, drip)
            while pieces:
                drip()

            @pl.when(hears)
            def _():
                near_ring.pass_on()
                near_forward(1)

        else:
            ring.pass_on()
            ring.collect(arrived)

        def pass_turn(m, j):
            turn_first(m, j).wait_recv()
            turn_second(m, j).start()

        def update(m, left, right, first, last, ship):
            def one(j, carry):
                at = block_at(j)
                fresh = inner_beta * moment[m, at, :] + contract(left[:, at], right[...], 0, 0)
                moment[m, at, :] = fresh
                moved = fresh if step == 0 else gone[m, at, :] + fresh
                gone[m, at, :] = moved
                if step < 2:
                    kept = weights[m, at, :] - learn_rate * fresh
                    weights[m, at, :] = kept
                if step == 0:

                    @pl.when(jnp.logical_not(ships))
                    def _():
                        out_box[0, m, at, :] = kept.astype(BF16)
                        turn_first(m, j).start()

                if step == 1:
                    out_box[1, m, at, :] = kept.astype(BF16)
                    ship(j).start()
                if step == 2:

                    @pl.when(core == 1 - m)
                    def _():
                        twin_out[at, :] = moved.astype(BF16)
                        twin_box(j).start()

                return carry

            lax.fori_loop(first, last, one, 0)

        def blend(m, at, other):
            mixed = 0.5 * (weights[m, at, :] + other)
            weights[m, at, :] = mixed
            cast[m, at, :] = mixed.astype(BF16)

        if step == 1:
            update(1, error.at[step], hidden, 0, 2, lambda j: leg(0, j))
            update(1, error.at[step], hidden, 2, 4, lambda j: box(1, j))
            update(0, inputs, back, 0, 4, lambda j: box(0, j))
        elif step == 0:
            update(1, error.at[step], hidden, 0, 4, None)

            @pl.when(jnp.logical_not(hears))
            def _():
                pass_turn(1, 0)
                pass_turn(1, 1)

            update(0, inputs, back, 0, 4, None)

            @pl.when(jnp.logical_not(hears))
            def _():
                pass_turn(1, 2)
                pass_turn(1, 3)
        else:
            @pl.when(core == 0)
            def _():
                update(1, error.at[step], hidden, 0, 4, None)
                update(0, inputs, back, 0, 4, None)

            @pl.when(core == 1)
            def _():
                update(0, inputs, back, 0, 4, None)
                update(1, error.at[step], hidden, 0, 4, None)

        ring.finish()

        if step == 0:

            @pl.when(ships)
            def _():
                for i in range(4):
                    near_x(i).wait_send()

            fetch(1)

            @pl.when(hears)
            def _():
                near_ring.collect(
                    lambda chunk: pull(near_error, chunk_at(chunk), near_slope, near_back)
                )
                for m in (1, 0):
                    for j in range(blocks):
                        near_m(m, j).wait_recv()
                for m, left, right in ((1, near_error, near_hidden), (0, near_inputs, near_back)):

                    def one(j, carry):
                        at = block_at(j)
                        grad = contract(left[:, at], right[...], 0, 0)
                        began = weights[m, at, :] + learn_rate * moment[m, at, :]
                        near = began - learn_rate * (in_box[0, m, at, :].astype(F32) + grad)
                        blend(m, at, near.astype(BF16).astype(F32))
                        return carry

                    lax.fori_loop(0, blocks, one, 0)
                near_ring.finish_gather()

            @pl.when(jnp.logical_not(hears))
            def _():
                def take_turn(m, j):
                    turn_second(m, j).wait_recv()
                    blend(m, block_at(j), in_box[0, m, block_at(j), :].astype(F32))

                pass_turn(0, 0)
                pass_turn(0, 1)
                take_turn(1, 0)
                pass_turn(0, 2)
                take_turn(1, 1)
                pass_turn(0, 3)
                take_turn(1, 2)
                take_turn(1, 3)
                for j in range(blocks):
                    take_turn(0, j)
            @pl.when(ships)
            def _():
                for m in (1, 0):
                    for j in range(blocks):
                        near_m(m, j).wait_send()
                near_shard().wait_send()

        if step == 1:

            def take(m, j, copy):
                copy.wait_recv()
                blend(m, block_at(j), in_box[1, m, block_at(j), :].astype(F32))

            def relay_on(hop_index, j):
                leg(hop_index, j).wait_recv()
                leg(hop_index + 1, j).start()

            fetch(2)
            relay_on(0, 0)
            relay_on(0, 1)
            take(1, 2, box(1, 2))
            relay_on(1, 0)
            take(1, 3, box(1, 3))
            relay_on(1, 1)
            take(0, 0, box(0, 0))
            take(0, 1, box(0, 1))
            take(1, 0, leg(2, 0))
            take(0, 2, box(0, 2))
            take(1, 1, leg(2, 1))
            take(0, 3, box(0, 3))
            for m, j in ((1, 2), (1, 3), (0, 0), (0, 1), (0, 2), (0, 3)):
                box(m, j).wait_send()
            for hop_index in range(3):
                for j in (0, 1):
                    leg(hop_index, j).wait_send()

            @pl.when(jnp.logical_not(ships))
            def _():
                for m in (1, 0):
                    for j in range(blocks):
                        turn_first(m, j).wait_send()

            @pl.when(jnp.logical_not(hears))
            def _():
                for m in (1, 0):
                    for j in range(blocks):
                        turn_second(m, j).wait_send()

    for step in range(INNER):
        one_step(step)

    store = pltpu.make_async_copy(moment, moment_out.at[0], local.at[2])
    store.start()

    ring = mean_ring

    def join(chunk):
        at = pl.ds(pl.multiple_of(chunk * tall, tall), tall)
        twin_box(chunk).wait_recv()
        both = gone[core, at, :] + twin_in[at, :].astype(F32)
        part2[chunk] = both.astype(BF16).reshape(2, tall // 2, units)

    summed = ring.reduce(join)
    own = pl.ds(pl.multiple_of((depth * 2 + low) * (width // 8), width // 8), width // 8)
    total[core, own, :] = summed.astype(BF16)

    def across(which, chunk):
        at = pl.ds(pl.multiple_of(chunk * tall, tall), tall)
        return pltpu.make_async_remote_copy(
            src_ref=total.at[which, at],
            dst_ref=total.at[which, at],
            send_sem=core_send.at[chunk],
            recv_sem=core_recv.at[chunk],
            device_id=twin,
            device_id_type=MESH,
        )

    ring.open()
    ring.pass_on()
    ring.collect(lambda chunk: across(core, chunk).start())
    saves = [
        pltpu.make_async_copy(total.at[which], total_out.at[which], local.at[place])
        for place, which in enumerate((core, 1 - core))
    ]
    saves[0].start()
    for chunk in range(4):
        across(1 - core, chunk).wait_recv()
    saves[1].start()
    for chunk in range(4):
        across(core, chunk).wait_send()
        twin_box(chunk).wait_send()
    ring.finish()
    for save in saves:
        save.wait()
    store.wait()


def body(tokens, targets, row_ids, anchor, momentum, slow):
    rows, width = tokens.shape
    units = anchor.shape[2]
    shard, wide = rows // 8, width // 8
    any_spec = pl.BlockSpec(memory_space=pl.ANY)
    hbm_spec = pl.BlockSpec(memory_space=pltpu.HBM)
    dma = pltpu.SemaphoreType.DMA
    ids = row_ids.reshape(INNER, 1, rows)
    ids, tokens, targets = (pltpu.with_memory_space_constraint(x, pltpu.HBM) for x in (ids, tokens, targets))
    moment, total = pl.pallas_call(
        kernel,
        name="outer_round",
        out_shape=(
            jax.ShapeDtypeStruct(momentum.shape, F32),
            jax.ShapeDtypeStruct(anchor.shape, BF16),
        ),
        in_specs=[hbm_spec] * 5,
        out_specs=(any_spec, any_spec),
        scratch_shapes=[
            pltpu.VMEM((INNER, 1, rows), jnp.int32),
            pltpu.VMEM((rows, width), BF16),
            pltpu.VMEM((rows, width), BF16),
            pltpu.VMEM((2, width, units), F32),
            pltpu.VMEM((2, width, units), F32),
            pltpu.VMEM((2, width, units), F32),
            pltpu.VMEM((2, width, units), BF16),
            pltpu.VMEM((2, 2, width, units), BF16),
            pltpu.VMEM((2, 2, width, units), BF16),
            pltpu.VMEM((width, units), BF16),
            pltpu.VMEM((width, units), BF16),
            pltpu.VMEM((rows, width), BF16),
            pltpu.VMEM((rows, units), BF16),
            pltpu.VMEM((rows, units), F32),
            pltpu.VMEM((rows, units), BF16),
            pltpu.VMEM((2, shard, width), F32),
            pltpu.VMEM((rows, width), BF16),
            pltpu.VMEM((rows, units), BF16),
            pltpu.VMEM((rows, units), F32),
            pltpu.VMEM((rows, units), BF16),
            pltpu.VMEM((rows, width), BF16),
            pltpu.VMEM((2, 2, width // 4, units), BF16),
            pltpu.VMEM((8, width // 4, units), BF16),
            pltpu.VMEM((4, 2, shard, width), BF16),
            pltpu.VMEM((INNER, 2, shard, width), BF16),
            pltpu.VMEM((2, shard, width), BF16),
            pltpu.VMEM((INNER, 2, 2, shard, width), BF16),
            pltpu.VMEM((shard, width), BF16),
            pltpu.VMEM((INNER, shard, width), BF16),
            pltpu.VMEM((INNER, rows, width), BF16),
            pltpu.VMEM((4, 2, wide, units), BF16),
            pltpu.VMEM((2, wide, units), BF16),
            pltpu.VMEM((2, wide, units), BF16),
            pltpu.VMEM((2, 2, wide, units), BF16),
            pltpu.VMEM((wide, units), BF16),
            pltpu.VMEM((wide, units), BF16),
            pltpu.VMEM((2, width, units), BF16),
            dma((INNER, 14)),
            dma((INNER, 14)),
            dma((14,)),
            dma((14,)),
            dma((14,)),
            dma((14,)),
            dma((8,)),
            dma((8,)),
            dma((13,)),
            dma((13,)),
            dma((16,)),
            dma((16,)),
            dma((3, 2)),
            dma((3, 2)),
            dma((4,)),
            dma((4,)),
            dma((4,)),
            dma((4,)),
            dma((6,)),
        ],
        compiler_params=pltpu.CompilerParams(
            collective_id=0, has_side_effects=True, vmem_limit_bytes=49 * 1024 * 1024
        ),
    )(ids, tokens, targets, anchor, momentum)
    mean = total.astype(F32) * (1.0 / lax.axis_size("replica"))
    slow_new = slow_beta * slow + mean
    anchor_new = anchor - learn_rate * slow_new
    return (anchor_new, slow_new, moment)


def solution(mesh):
    return jax.shard_map(
        body,
        mesh=mesh,
        in_specs=(
            P("replica", None),
            P("replica", None),
            P("replica", None, None),
            P(None, None, "tensor"),
            P("replica", None, None, "tensor"),
            P(None, None, "tensor"),
        ),
        out_specs=(
            P(None, None, "tensor"),
            P(None, None, "tensor"),
            P("replica", None, None, "tensor"),
        ),
        check_vma=False,
    )
```

```python
import functools

import jax
import jax.numpy as jnp
from jax import lax
from jax.experimental import pallas as pl
from jax.experimental.pallas import tpu as pltpu
from jax.sharding import PartitionSpec as P

INNER = 3
learn_rate = 0.02
inner_beta = 0.9
slow_beta = 0.5

F32 = jnp.float32
BF16 = jnp.bfloat16
MESH = pl.DeviceIdType.MESH


def gelu_pair(pre):
    coeff = 0.7978845608028654
    square = pre * pre
    tanh_val = jnp.tanh(coeff * (pre + 0.044715 * pre * square))
    upper = 0.5 * (1.0 + tanh_val)
    value = pre * upper
    slope = upper + 0.5 * pre * (1.0 - tanh_val * tanh_val) * coeff * (
        1.0 + 3.0 * 0.044715 * square
    )
    return (value, slope)


def contract(a, b, dim_a, dim_b):
    return lax.dot_general(a, b, (((dim_a,), (dim_b,)), ((), ())), preferred_element_type=F32)


class Exchange:
    def __init__(self, pos, half, at, block, part, hop, mid, fin, give, got, full, send, recv):
        self.pos, self.half, self.block = pos, half, block
        self.part, self.hop, self.mid, self.fin = part, hop, mid, fin
        self.give, self.got, self.full, self.send, self.recv = give, got, full, send, recv
        self.far, self.above, self.below = (pos + 2) % 4, (pos + 1) % 4, (pos + 3) % 4
        self.first_of = at(self.above, 0)
        self.second_of = at(self.below, 1)
        self.up, self.down = at(self.above, half), at(self.below, half)
        self.up_across, self.down_across = at(self.above, 1 - half), at(self.below, 1 - half)
        self.pair = at(pos, 1 - half)
        self.sent = []

    def peers(self):
        return [self.up, self.down, self.up_across, self.down_across, self.pair]

    def copy(self, src, dst, index, device, landing=None):
        return pltpu.make_async_remote_copy(
            src_ref=src,
            dst_ref=dst,
            send_sem=self.send.at[index],
            recv_sem=self.recv.at[index if landing is None else landing],
            device_id=device,
            device_id_type=MESH,
        )

    def start(self, src, dst, index, device, landing=None):
        copy = self.copy(src, dst, index, device, landing)
        copy.start()
        self.sent.append(copy)
        return copy

    def reduce(self, make, idle=None, between=lambda: None):
        pos, half, part, fin, mid = self.pos, self.half, self.part, self.fin, self.mid
        make(self.far)
        first_up = self.start(part.at[self.far, 0], self.hop.at[0], 0, self.up)
        first_down = self.start(part.at[self.far, 1], self.hop.at[1], 1, self.down)
        between()
        make(self.above)
        direct_up = self.start(part.at[self.above, 1], fin.at[1, 0], 2, self.up)
        between()
        make(self.below)
        direct_down = self.start(part.at[self.below, 0], fin.at[0, 0], 3, self.down)
        between()
        make(pos)
        between()
        first_up.wait_recv()
        mid[0] = (part[self.above, 0].astype(F32) + self.hop[0].astype(F32)).astype(BF16)
        self.start(mid.at[0], fin.at[half, 1], 4, self.first_of, 4 + half)
        first_down.wait_recv()
        mid[1] = (part[self.below, 1].astype(F32) + self.hop[1].astype(F32)).astype(BF16)
        self.start(mid.at[1], fin.at[half, 1], 5, self.second_of, 4 + half)
        if idle is not None:
            idle()
        direct_up.wait_recv()
        direct_down.wait_recv()
        self.give[...] = self.near_total(1 - half).astype(BF16)
        last = self.start(self.give, self.got, 6, self.pair)
        mine = self.near_total(half)
        for plane in (0, 1):
            self.copy(mid.at[0], fin.at[plane, 1], 4, self.first_of, 4 + plane).wait_recv()
        mine = mine + fin[0, 1].astype(F32) + fin[1, 1].astype(F32)
        last.wait_recv()
        return mine + self.got[...].astype(F32)

    def near_total(self, half):
        return self.part[self.pos, half].astype(F32) + self.fin[half, 0].astype(F32)

    def slot(self, chunk, half):
        return self.full.at[pl.ds(pl.multiple_of((chunk * 2 + half) * self.block, self.block), self.block)]

    def open(self):
        own = self.slot(self.pos, self.half)
        self.start(own, own, 8, self.up)
        self.start(own, own, 9, self.down)
        self.start(own, own, 11, self.down_across)
        self.start(own, own, 10, self.up_across)
        self.start(own, own, 7, self.pair)

    def await_slot(self, chunk, half, index):
        slot = self.slot(chunk, half)
        self.copy(slot, slot, index, self.pair).wait_recv()
        return slot

    def pass_on(self):
        early = self.await_slot(self.below, self.half, 8)
        self.start(early, early, 12, self.up)
        late = self.await_slot(self.above, 1 - self.half, 11)
        self.start(late, late, 13, self.down)

    def collect(self, arrived, between=lambda: None):
        half = self.half
        self.await_slot(self.pos, 1 - half, 7)
        arrived(self.pos)
        between()
        self.await_slot(self.above, half, 9)
        arrived(self.above)
        between()
        self.await_slot(self.below, 1 - half, 10)
        arrived(self.below)
        between()
        self.await_slot(self.far, half, 12)
        self.await_slot(self.far, 1 - half, 13)
        arrived(self.far)

    def finish(self):
        for copy in self.sent:
            copy.wait_send()

    def finish_gather(self):
        for index in range(7, 14):
            slot = self.slot(self.pos, self.half)
            self.copy(slot, slot, index, self.pair).wait_send()


def kernel(
    ids_far, tokens_far, targets_far, anchor, momentum,
    moment_out, total_out,
    ids, tokens, targets, weights, moment, gone, cast, out_box, in_box, twin_out, twin_in,
    inputs, hidden, slope, back, want,
    near_inputs, near_hidden, near_slope, near_back, near_error, relay, carried,
    part, hop, mid, fin, give, got, error,
    part2, hop2, mid2, fin2, give2, got2, total,
    send, recv, send2, recv2, send3, recv3, box_send, box_recv, near_send, near_recv, turn_send, turn_recv,
    relay_send, relay_recv, twin_send, twin_recv, core_send, core_recv, local,
):
    rep, ten = lax.axis_index("replica"), lax.axis_index("tensor")
    row, side = ten // 2, ten % 2
    low, depth, core = rep // 8, (rep // 2) % 4, rep % 2

    def plane(shift):
        return low * 8 + (depth + shift) % 4 * 2 + core

    def tensor_at(pos, half):
        return (rep, pos * 2 + half)

    def mean_at(pos, half):
        return (half * 8 + pos * 2 + core, ten)

    up2, down2 = (plane(1), ten), (plane(3), ten)
    twin = (low * 8 + depth * 2 + 1 - core, ten)
    after, second = ((rep + 1) % 16, ten), ((rep + 2) % 16, ten)
    relay_end = ((plane(2) + 2) % 16, ten)
    past = (rep + 14) % 16
    ships = (depth != 3) | (core != 1)
    hears = (depth != 0) | (core != 0)
    turner = (low * 8 + (depth + 1) % 4 * 2 + 1 - core, ten)
    turned = (low * 8 + (depth + 3) % 4 * 2 + 1 - core, ten)
    beside = ((1 - low) * 8 + depth * 2 + core, ten)
    relay_start = (past // 8 * 8 + ((past // 2) % 4 + 2) % 4 * 2 + core, ten)

    load = [
        pltpu.make_async_copy(anchor.at[0], weights.at[0], local.at[0]),
        pltpu.make_async_copy(anchor.at[1], weights.at[1], local.at[1]),
        pltpu.make_async_copy(momentum.at[0], moment, local.at[2]),
        pltpu.make_async_copy(targets_far, targets, local.at[5]),
    ]
    first_load = [
        pltpu.make_async_copy(ids_far, ids, local.at[3]),
        pltpu.make_async_copy(tokens_far, tokens, local.at[4]),
    ]
    for copy in first_load:
        copy.start()
    for copy in load:
        copy.start()

    shard_rows = inputs.shape[0] // 8
    mean_ring = Exchange(
        depth, low, mean_at, inputs.shape[1] // 8, part2, hop2, mid2, fin2,
        give2, got2, total.at[core], send2, recv2,
    )
    rings = [
        Exchange(
            row, side, tensor_at, shard_rows, part, hop.at[step], mid, fin.at[step],
            give, got.at[step], error.at[step], send.at[step], recv.at[step],
        )
        for step in range(INNER)
    ]
    near_ring = Exchange(
        row, side, tensor_at, shard_rows, part, None, mid, None,
        give, None, near_error, send3, recv3,
    )
    barrier = pltpu.get_barrier_semaphore()
    peers = rings[0].peers() + mean_ring.peers() + [twin, relay_end, relay_start, turner, turned]
    peers += [((rep + shift) % 16, ten) for shift in (1, 2, 14, 15)]
    for peer in peers:
        pl.semaphore_signal(barrier, inc=1, device_id=peer, device_id_type=MESH)

    rows, width = inputs.shape
    units = hidden.shape[1]
    blocks = 4
    tall = width // blocks
    chunk_rows = rows // 4

    def remote(src, dst, send_sem, recv_sem, device):
        return pltpu.make_async_remote_copy(
            src_ref=src, dst_ref=dst, send_sem=send_sem, recv_sem=recv_sem,
            device_id=device, device_id_type=MESH,
        )

    def chunk_at(chunk):
        return pl.ds(pl.multiple_of(chunk * chunk_rows, chunk_rows), chunk_rows)

    def block_at(j):
        return pl.ds(pl.multiple_of(j * tall, tall), tall)

    def picked(step, chunk, table):
        chosen = ids[step, :, chunk_at(chunk)]
        places = lax.broadcasted_iota(jnp.int32, (rows, chunk_rows), 0)
        mask = jnp.where(chosen == places, 1.0, 0.0).astype(BF16)
        return contract(mask, table[...], 0, 0)

    def fetch(step):
        def some(i, carry):
            inputs[chunk_at(i), :] = picked(step, i, tokens).astype(BF16)
            return carry

        lax.fori_loop(0, 4, some, 0)

    def start_cast(i, carry):
        at = pl.ds(pl.multiple_of(i * 128, 128), 128)
        for m in (0, 1):
            cast[m, at, :] = weights[m, at, :].astype(BF16)
        return carry

    def near_x(i):
        at = chunk_at(i)
        return remote(inputs.at[at], near_inputs.at[at], near_send.at[8 + i], near_recv.at[8 + i], after)

    def near_m(m, j):
        at = block_at(j)
        index = m * blocks + j
        return remote(
            out_box.at[0, m, at], in_box.at[0, m, at], near_send.at[index], near_recv.at[index], after
        )

    def near_shard():
        own = pl.ds(pl.multiple_of(ten * shard_rows, shard_rows), shard_rows)
        return remote(error.at[0, own], near_error.at[own], near_send.at[12], near_recv.at[12], after)

    pieces = [("x", 0, i) for i in range(4)] + [("m", m, j) for m in (1, 0) for j in range(4)]

    def drip():
        if not pieces:
            return
        kind, m, j = pieces.pop(0)
        if (kind, m, j) == ("m", 1, 0):
            load[2].wait()

        @pl.when(ships)
        def _():
            if kind == "x":
                near_x(j).start()
                return

            def decay(i, carry):
                at = pl.ds(pl.multiple_of(j * tall + i * 64, 64), 64)
                out_box[0, m, at, :] = (inner_beta * moment[m, at, :]).astype(BF16)
                return carry

            lax.fori_loop(0, tall // 64, decay, 0)
            near_m(m, j).start()

    def turn_first(m, j):
        place = m * blocks + j
        return remote(
            out_box.at[0, m, block_at(j)], carried.at[place],
            turn_send.at[place], turn_recv.at[8 + place], turner,
        )

    def straight(m, j):
        at, place = block_at(j), m * blocks + j
        return remote(
            out_box.at[0, m, at], in_box.at[0, m, at], turn_send.at[place], turn_recv.at[place], after
        )

    def turn_second(m, j):
        place = m * blocks + j
        return remote(
            carried.at[place], in_box.at[0, m, block_at(j)],
            turn_send.at[8 + place], turn_recv.at[place], beside,
        )

    def box(m, j):
        at = block_at(j)
        index = m * blocks + j
        return remote(
            out_box.at[1, m, at], in_box.at[1, m, at], box_send.at[index], box_recv.at[index], second
        )

    def leg(hop_index, j):
        src = out_box.at[1, 1, block_at(j)] if hop_index == 0 else relay.at[hop_index - 1, j]
        dst = in_box.at[1, 1, block_at(j)] if hop_index == 2 else relay.at[hop_index, j]
        return remote(
            src, dst, relay_send.at[hop_index, j], relay_recv.at[hop_index, j],
            relay_end if hop_index == 2 else down2,
        )

    def twin_box(j):
        at = block_at(j)
        return remote(twin_out.at[at], twin_in.at[at], twin_send.at[j], twin_recv.at[j], twin)

    for copy in first_load:
        copy.wait()
    fetch(0)
    load[0].wait()
    load[1].wait()
    lax.fori_loop(0, width // 128, start_cast, 0)
    pl.semaphore_wait(barrier, len(peers))
    drip()

    def one_step(step):
        ring = rings[step]

        def forward(source, at, kept, rise):
            pre = jnp.dot(source[at, :], cast[0], preferred_element_type=F32)
            value, tilt = gelu_pair(pre)
            value = value.astype(BF16)
            kept[at, :] = value
            rise[at, :] = tilt
            return value

        def make(chunk):
            value = forward(inputs, chunk_at(chunk), hidden, slope)
            out = contract(value, cast[1], 1, 1)
            part[chunk] = out.astype(BF16).reshape(2, shard_rows, width)

        def idle():
            if step == 0:
                load[3].wait()
            want[...] = picked(step, row, targets).reshape(2, shard_rows, width)

        summed = ring.reduce(make, idle, drip if step == 0 else lambda: None)
        own = pl.ds(pl.multiple_of(ten * shard_rows, shard_rows), shard_rows)
        error[step, own, :] = ((summed - want[side]) * (1.0 / rows)).astype(BF16)

        def pull(source, at, rise, result):
            slide = jnp.dot(source[at, :], cast[1], preferred_element_type=F32)
            result[at, :] = (slide * rise[at, :]).astype(BF16)

        def arrived(chunk):
            pull(error.at[step], chunk_at(chunk), slope, back)

        def near_forward(part_of):
            for i in (part_of * 2, part_of * 2 + 1):
                near_x(i).wait_recv()

            def one(i, carry):
                forward(near_inputs, chunk_at(i), near_hidden, near_slope)
                return carry

            lax.fori_loop(part_of * 2, part_of * 2 + 2, one, 0)

        ring.open()
        if step == 0:

            @pl.when(ships)
            def _():
                near_shard().start()

            drip()

            @pl.when(hears)
            def _():
                near_forward(0)

            drip()
            ring.pass_on()

            @pl.when(hears)
            def _():
                near_shard().wait_recv()
                near_ring.open()

            drip()
            ring.collect(arrived, drip)
            while pieces:
                drip()

            @pl.when(hears)
            def _():
                near_ring.pass_on()
                near_forward(1)

        else:
            ring.pass_on()
            ring.collect(arrived)

        def pass_turn(m, j):
            turn_first(m, j).wait_recv()
            turn_second(m, j).start()

        def update(m, left, right, first, last, ship):
            def one(j, carry):
                at = block_at(j)
                fresh = inner_beta * moment[m, at, :] + contract(left[:, at], right[...], 0, 0)
                moment[m, at, :] = fresh
                moved = fresh if step == 0 else gone[m, at, :] + fresh
                gone[m, at, :] = moved
                if step < 2:
                    kept = weights[m, at, :] - learn_rate * fresh
                    weights[m, at, :] = kept
                if step == 0:

                    @pl.when(jnp.logical_not(ships))
                    def _():
                        out_box[0, m, at, :] = kept.astype(BF16)
                        if m == 1:
                            turn_first(m, j).start()
                        else:

                            @pl.when(j < 2)
                            def _():
                                turn_first(m, j).start()

                            @pl.when(j >= 2)
                            def _():
                                straight(m, j).start()

                if step == 1:
                    out_box[1, m, at, :] = kept.astype(BF16)
                    ship(j).start()
                if step == 2:

                    @pl.when(core == 1 - m)
                    def _():
                        twin_out[at, :] = moved.astype(BF16)
                        twin_box(j).start()

                return carry

            lax.fori_loop(first, last, one, 0)

        def blend(m, at, other):
            mixed = 0.5 * (weights[m, at, :] + other)
            weights[m, at, :] = mixed
            cast[m, at, :] = mixed.astype(BF16)

        if step == 1:
            update(1, error.at[step], hidden, 0, 2, lambda j: leg(0, j))
            update(1, error.at[step], hidden, 2, 4, lambda j: box(1, j))
            update(0, inputs, back, 0, 4, lambda j: box(0, j))
        elif step == 0:
            update(1, error.at[step], hidden, 0, 4, None)

            @pl.when(jnp.logical_not(hears))
            def _():
                pass_turn(1, 0)
                pass_turn(1, 1)

            update(0, inputs, back, 0, 4, None)

            @pl.when(jnp.logical_not(hears))
            def _():
                pass_turn(1, 2)
                pass_turn(1, 3)
        else:
            @pl.when(core == 0)
            def _():
                update(1, error.at[step], hidden, 0, 4, None)
                update(0, inputs, back, 0, 4, None)

            @pl.when(core == 1)
            def _():
                update(0, inputs, back, 0, 4, None)
                update(1, error.at[step], hidden, 0, 4, None)

        ring.finish()

        if step == 0:

            @pl.when(ships)
            def _():
                for i in range(4):
                    near_x(i).wait_send()

            fetch(1)

            @pl.when(hears)
            def _():
                near_ring.collect(
                    lambda chunk: pull(near_error, chunk_at(chunk), near_slope, near_back)
                )
                for m in (1, 0):
                    for j in range(blocks):
                        near_m(m, j).wait_recv()
                for m, left, right in ((1, near_error, near_hidden), (0, near_inputs, near_back)):

                    def one(j, carry):
                        at = block_at(j)
                        grad = contract(left[:, at], right[...], 0, 0)
                        began = weights[m, at, :] + learn_rate * moment[m, at, :]
                        near = began - learn_rate * (in_box[0, m, at, :].astype(F32) + grad)
                        blend(m, at, near.astype(BF16).astype(F32))
                        return carry

                    lax.fori_loop(0, blocks, one, 0)
                near_ring.finish_gather()

            @pl.when(jnp.logical_not(hears))
            def _():
                def take_turn(m, j):
                    turn_second(m, j).wait_recv()
                    blend(m, block_at(j), in_box[0, m, block_at(j), :].astype(F32))

                pass_turn(0, 0)
                pass_turn(0, 1)
                take_turn(1, 0)
                take_turn(1, 1)
                take_turn(1, 2)
                take_turn(1, 3)
                for j in range(blocks):
                    take_turn(0, j)
            @pl.when(ships)
            def _():
                for m in (1, 0):
                    for j in range(blocks):
                        near_m(m, j).wait_send()
                near_shard().wait_send()

        if step == 1:

            def take(m, j, copy):
                copy.wait_recv()
                blend(m, block_at(j), in_box[1, m, block_at(j), :].astype(F32))

            def relay_on(hop_index, j):
                leg(hop_index, j).wait_recv()
                leg(hop_index + 1, j).start()

            fetch(2)
            relay_on(0, 0)
            relay_on(0, 1)
            take(1, 2, box(1, 2))
            relay_on(1, 0)
            take(1, 3, box(1, 3))
            relay_on(1, 1)
            take(0, 0, box(0, 0))
            take(0, 1, box(0, 1))
            take(1, 0, leg(2, 0))
            take(0, 2, box(0, 2))
            take(1, 1, leg(2, 1))
            take(0, 3, box(0, 3))
            for m, j in ((1, 2), (1, 3), (0, 0), (0, 1), (0, 2), (0, 3)):
                box(m, j).wait_send()
            for hop_index in range(3):
                for j in (0, 1):
                    leg(hop_index, j).wait_send()

            @pl.when(jnp.logical_not(ships))
            def _():
                for m in (1, 0):
                    for j in range(blocks):
                        turn_first(m, j).wait_send()

            @pl.when(jnp.logical_not(hears))
            def _():
                for m in (1, 0):
                    for j in range(blocks if m == 1 else 2):
                        turn_second(m, j).wait_send()

    for step in range(INNER):
        one_step(step)

    store = pltpu.make_async_copy(moment, moment_out.at[0], local.at[2])
    store.start()

    ring = mean_ring

    def join(chunk):
        at = pl.ds(pl.multiple_of(chunk * tall, tall), tall)
        twin_box(chunk).wait_recv()
        both = gone[core, at, :] + twin_in[at, :].astype(F32)
        part2[chunk] = both.astype(BF16).reshape(2, tall // 2, units)

    summed = ring.reduce(join)
    own = pl.ds(pl.multiple_of((depth * 2 + low) * (width // 8), width // 8), width // 8)
    total[core, own, :] = summed.astype(BF16)

    def across(which, chunk):
        at = pl.ds(pl.multiple_of(chunk * tall, tall), tall)
        return pltpu.make_async_remote_copy(
            src_ref=total.at[which, at],
            dst_ref=total.at[which, at],
            send_sem=core_send.at[chunk],
            recv_sem=core_recv.at[chunk],
            device_id=twin,
            device_id_type=MESH,
        )

    ring.open()
    ring.pass_on()
    ring.collect(lambda chunk: across(core, chunk).start())
    saves = [
        pltpu.make_async_copy(total.at[which], total_out.at[which], local.at[place])
        for place, which in enumerate((core, 1 - core))
    ]
    saves[0].start()
    for chunk in range(4):
        across(1 - core, chunk).wait_recv()
    saves[1].start()
    for chunk in range(4):
        across(core, chunk).wait_send()
        twin_box(chunk).wait_send()
    ring.finish()
    for save in saves:
        save.wait()
    store.wait()


def body(tokens, targets, row_ids, anchor, momentum, slow):
    rows, width = tokens.shape
    units = anchor.shape[2]
    shard, wide = rows // 8, width // 8
    any_spec = pl.BlockSpec(memory_space=pl.ANY)
    hbm_spec = pl.BlockSpec(memory_space=pltpu.HBM)
    dma = pltpu.SemaphoreType.DMA
    ids = row_ids.reshape(INNER, 1, rows)
    ids, tokens, targets = (pltpu.with_memory_space_constraint(x, pltpu.HBM) for x in (ids, tokens, targets))
    moment, total = pl.pallas_call(
        kernel,
        name="outer_round",
        out_shape=(
            jax.ShapeDtypeStruct(momentum.shape, F32),
            jax.ShapeDtypeStruct(anchor.shape, BF16),
        ),
        in_specs=[hbm_spec] * 5,
        out_specs=(any_spec, any_spec),
        scratch_shapes=[
            pltpu.VMEM((INNER, 1, rows), jnp.int32),
            pltpu.VMEM((rows, width), BF16),
            pltpu.VMEM((rows, width), BF16),
            pltpu.VMEM((2, width, units), F32),
            pltpu.VMEM((2, width, units), F32),
            pltpu.VMEM((2, width, units), F32),
            pltpu.VMEM((2, width, units), BF16),
            pltpu.VMEM((2, 2, width, units), BF16),
            pltpu.VMEM((2, 2, width, units), BF16),
            pltpu.VMEM((width, units), BF16),
            pltpu.VMEM((width, units), BF16),
            pltpu.VMEM((rows, width), BF16),
            pltpu.VMEM((rows, units), BF16),
            pltpu.VMEM((rows, units), F32),
            pltpu.VMEM((rows, units), BF16),
            pltpu.VMEM((2, shard, width), F32),
            pltpu.VMEM((rows, width), BF16),
            pltpu.VMEM((rows, units), BF16),
            pltpu.VMEM((rows, units), F32),
            pltpu.VMEM((rows, units), BF16),
            pltpu.VMEM((rows, width), BF16),
            pltpu.VMEM((2, 2, width // 4, units), BF16),
            pltpu.VMEM((8, width // 4, units), BF16),
            pltpu.VMEM((4, 2, shard, width), BF16),
            pltpu.VMEM((INNER, 2, shard, width), BF16),
            pltpu.VMEM((2, shard, width), BF16),
            pltpu.VMEM((INNER, 2, 2, shard, width), BF16),
            pltpu.VMEM((shard, width), BF16),
            pltpu.VMEM((INNER, shard, width), BF16),
            pltpu.VMEM((INNER, rows, width), BF16),
            pltpu.VMEM((4, 2, wide, units), BF16),
            pltpu.VMEM((2, wide, units), BF16),
            pltpu.VMEM((2, wide, units), BF16),
            pltpu.VMEM((2, 2, wide, units), BF16),
            pltpu.VMEM((wide, units), BF16),
            pltpu.VMEM((wide, units), BF16),
            pltpu.VMEM((2, width, units), BF16),
            dma((INNER, 14)),
            dma((INNER, 14)),
            dma((14,)),
            dma((14,)),
            dma((14,)),
            dma((14,)),
            dma((8,)),
            dma((8,)),
            dma((13,)),
            dma((13,)),
            dma((16,)),
            dma((16,)),
            dma((3, 2)),
            dma((3, 2)),
            dma((4,)),
            dma((4,)),
            dma((4,)),
            dma((4,)),
            dma((6,)),
        ],
        compiler_params=pltpu.CompilerParams(
            collective_id=0, has_side_effects=True, vmem_limit_bytes=49 * 1024 * 1024
        ),
    )(ids, tokens, targets, anchor, momentum)
    mean = total.astype(F32) * (1.0 / lax.axis_size("replica"))
    slow_new = slow_beta * slow + mean
    anchor_new = anchor - learn_rate * slow_new
    return (anchor_new, slow_new, moment)


def solution(mesh):
    return jax.shard_map(
        body,
        mesh=mesh,
        in_specs=(
            P("replica", None),
            P("replica", None),
            P("replica", None, None),
            P(None, None, "tensor"),
            P("replica", None, None, "tensor"),
            P(None, None, "tensor"),
        ),
        out_specs=(
            P(None, None, "tensor"),
            P(None, None, "tensor"),
            P("replica", None, None, "tensor"),
        ),
        check_vma=False,
    )
```
